32 devices in a mesh: dp: 8 (over z, x), mp: 4 (over y, core).
Axes of the slice: x: 2, y: 2, z: 4, core: 2. Of those that a mesh axis runs over, the one named last changes fastest.
Arguments:
- features: bfloat16 [8192, 1024], P('dp'), may hold values from -6 to 6
- out_grads: bfloat16 [8192, 4, 1024], P('dp', None, 'mp'), may hold values from -0.0625 to 0.0625
- norm_grads: float32 [8, 2048], P('dp'), may hold values from -2 to 2
- owners: int32 [5], replicated, may hold values from 0 to 7, as said below
- moment1: float32 [4, 1024, 1024], P(None, 'dp', 'mp'), may hold values from -6 to 6
- moment2: float32 [4, 1024, 1024], P(None, 'dp', 'mp'), may hold values from 0.1 to 10
- left_stats: float32 [4, 1024, 1024], P(None, 'dp', 'mp'), may hold values from -1024 to 1024, as said below
- right_stats: float32 [4, 1024, 1024], P(None, 'dp', 'mp'), may hold values from -1024 to 1024, as said below
- left_basis: float32 [4, 1024, 1024], P(None, 'dp', 'mp'), may hold values from -1 to 2
- right_basis: float32 [4, 1024, 1024], P(None, 'dp', 'mp'), may hold values from -1 to 2
- norm_m: float32 [2048], P('dp'), may hold values from -6 to 6
- norm_v: float32 [2048], P('dp'), may hold values from 0.1 to 10
Outputs:
- new_moment1: float32 [4, 1024, 1024], P(None, 'dp', 'mp')
- new_moment2: float32 [4, 1024, 1024], P(None, 'dp', 'mp')
- new_left_stats: float32 [4, 1024, 1024], P(None, 'dp', 'mp')
- new_right_stats: float32 [4, 1024, 1024], P(None, 'dp', 'mp')
- new_left_basis: float32 [4, 1024, 1024], P(None, 'dp', 'mp')
- new_right_basis: float32 [4, 1024, 1024], P(None, 'dp', 'mp')
- update_slots: bfloat16 [8, 1024, 1024], P('dp', None, 'mp')
- new_norm_m: float32 [2048], P('dp')
- new_norm_v: float32 [2048], P('dp')
- norm_slots: float32 [8, 2048], P('dp')
The draws below stay inside these ranges and needn't reach their ends.
Inputs may be any that keep to these rules, and one draw needn't show every extreme that they name: `owners`: the first 4 entries are distinct, so a dp index owns at most one tile; the last entry may equal any of them. `left_stats`: each tile of statistics is symmetric. `right_stats`: each tile of statistics is symmetric.
All inputs are finite; a program needn't handle non-finite values.
Results may differ from the reference program's by a relative error of at most 0.0072.
Values may be sent and summed in bfloat16 or wider, within the bound.
A program may use at most 128 MiB of HBM per device.

```python
import math
import jax
import jax.numpy as jnp
from jax import lax

D = 2048
TILE = 1024
NT = 4
TOKENS = 8192
N_DP = 8


def stats_single(key):
    key_diag, key_noise = jax.random.split(key)
    diag = TILE * jnp.exp(jax.random.uniform(key_diag, (TILE,), jnp.float32, math.log(0.1), 0.0))
    noise = jax.random.normal(key_noise, (TILE, TILE), jnp.float32)
    symmetric = (noise + noise.T) * 0.70710678
    scale = jnp.sqrt(diag[:, None] * diag[None, :]) * (0.3 / math.sqrt(TILE))
    positions = jnp.arange(TILE, dtype=jnp.int32)
    on_diag = positions[:, None] == positions[None, :]
    return jnp.where(on_diag, diag[:, None], scale * symmetric)


def basis_single(key):
    noise = jax.random.normal(key, (TILE, TILE), jnp.float32)
    positions = jnp.arange(TILE, dtype=jnp.int32)
    on_diag = (positions[:, None] == positions[None, :]).astype(jnp.float32)
    return on_diag + noise * (0.3 / math.sqrt(TILE))


def draw_owners(key, part):
    key_perm, key_mix, key_norm = jax.random.split(jax.random.fold_in(key, 5), 3)
    middle = (1 + jax.random.permutation(key_perm, N_DP - 2)[:NT - 2]).astype(jnp.int32)
    ends = jnp.array([0, N_DP - 1], dtype=jnp.int32)
    tiles = jax.random.permutation(key_mix, jnp.concatenate([ends, middle])).astype(jnp.int32)
    norm_owner = jax.random.randint(key_norm, (1,), 0, N_DP).astype(jnp.int32)
    return jnp.concatenate([tiles, norm_owner]).astype(jnp.int32)


def draw_left_stats(key, part):
    return jax.vmap(stats_single)(jax.random.split(jax.random.fold_in(key, 11), NT))


def draw_right_stats(key, part):
    return jax.vmap(stats_single)(jax.random.split(jax.random.fold_in(key, 13), NT))


def draw_left_basis(key, part):
    return jax.vmap(basis_single)(jax.random.split(jax.random.fold_in(key, 17), NT))


def draw_right_basis(key, part):
    return jax.vmap(basis_single)(jax.random.split(jax.random.fold_in(key, 19), NT))


def block_levels(stream_key, shape, cuts, low, top_value):
    gain = 1.0
    for dim, shards_of in cuts:
        heights = jax.random.uniform(jax.random.fold_in(jax.random.fold_in(stream_key, 6), dim), (shards_of,), jnp.float32, low / len(cuts), top_value / len(cuts))
        gain = gain * jnp.repeat(jnp.exp(heights), shape[dim] // shards_of).reshape((-1,) + (1,) * (len(shape) - 1 - dim))
    return gain


def gaussian(key, extent, scale, reach, pieces=(), kind=jnp.bfloat16):
    gain = block_levels(key, extent, pieces, -0.22, 0.18) if pieces else 1.0
    values = jax.random.normal(key, extent, jnp.float32) * scale * gain
    return jnp.minimum(jnp.maximum(values, -reach), reach).astype(kind)


def setup_inputs(seed: int = 0) -> dict:
    streams_of = jax.random.split(jax.random.key(seed), 13)
    return {
        "features": gaussian(streams_of[0], (TOKENS, TILE), 1.0, 6.0, ((0, 8),)),
        "out_grads": gaussian(streams_of[1], (TOKENS, NT, TILE), TOKENS ** -0.5, 0.0625, ((0, 8), (2, 4))),
        "norm_grads": gaussian(streams_of[2], (N_DP, D), N_DP ** -0.5, 2.0, ((0, 8),), jnp.float32),
        "owners": draw_owners(jax.random.fold_in(streams_of[12], 71), 0),
        "moment1": gaussian(streams_of[4], (NT, TILE, TILE), 1.0, 6.0, ((1, 8), (2, 4)), jnp.float32),
        "moment2": jnp.clip(jnp.exp(math.log(10.0) - 4.6051702 * jax.random.uniform(streams_of[5], (NT, TILE, TILE), jnp.float32) ** block_levels(streams_of[5], (NT, TILE, TILE), ((1, 8), (2, 4)), -0.2, 0.2)), 0.1, 10.0),
        "left_stats": draw_left_stats(jax.random.fold_in(streams_of[12], 71), 0),
        "right_stats": draw_right_stats(jax.random.fold_in(streams_of[12], 71), 0),
        "left_basis": draw_left_basis(jax.random.fold_in(streams_of[12], 71), 0),
        "right_basis": draw_right_basis(jax.random.fold_in(streams_of[12], 71), 0),
        "norm_m": gaussian(streams_of[10], (D,), 1.0, 6.0, ((0, 8),), jnp.float32),
        "norm_v": jnp.clip(jnp.exp(math.log(10.0) - 4.6051702 * jax.random.uniform(streams_of[11], (D,), jnp.float32) ** block_levels(streams_of[11], (D,), ((0, 8),), -0.2, 0.2)), 0.1, 10.0),
    }


FIX_ONE = 1.0 - 0.9 ** 10
FIX_TWO = 1.0 - 0.95 ** 10

def contract(left, right, left_dim, right_dim):
    return lax.dot_general(left, right, (((left_dim,), (right_dim,)), ((), ())), preferred_element_type=jnp.float32)

def reference(features, out_grads, norm_grads, owners, moment1, moment2, left_stats, right_stats, left_basis, right_basis, norm_m, norm_v):

    def tile_step(items):
        index, mom_one, mom_two, stats_l, stats_r, basis_l, basis_r = items
        grad_cols = lax.dynamic_index_in_dim(out_grads, index, 1, keepdims=False)
        grad = contract(features, grad_cols, 0, 0)
        grad_b = grad.astype(jnp.bfloat16)
        left_b = basis_l.astype(jnp.bfloat16)
        right_b = basis_r.astype(jnp.bfloat16)
        inner = jnp.dot(grad_b, right_b, preferred_element_type=jnp.float32).astype(jnp.bfloat16)
        rotated = contract(left_b, inner, 0, 0)
        new_one = 0.9 * mom_one + 0.1 * rotated
        new_two = 0.95 * mom_two + 0.05 * rotated * rotated
        direction = (new_one / FIX_ONE / (jnp.sqrt(new_two / FIX_TWO) + 1e-08)).astype(jnp.bfloat16)
        back = contract(direction, right_b, 1, 1).astype(jnp.bfloat16)
        update = jnp.dot(left_b, back, preferred_element_type=jnp.float32).astype(jnp.bfloat16)
        new_sl = 0.95 * stats_l + 0.05 * contract(grad_b, grad_b, 1, 1)
        new_sr = 0.95 * stats_r + 0.05 * contract(grad_b, grad_b, 0, 0)
        power_l = jnp.dot(new_sl.astype(jnp.bfloat16), left_b, preferred_element_type=jnp.float32)
        power_r = jnp.dot(new_sr.astype(jnp.bfloat16), right_b, preferred_element_type=jnp.float32)
        iter_l = (power_l * lax.rsqrt(lax.optimization_barrier(jnp.sum(power_l * power_l, axis=0, keepdims=True)) + 1e-06)).astype(jnp.bfloat16)
        iter_r = (power_r * lax.rsqrt(lax.optimization_barrier(jnp.sum(power_r * power_r, axis=0, keepdims=True)) + 1e-06)).astype(jnp.bfloat16)
        gram_l = contract(iter_l, iter_l, 0, 0).astype(jnp.bfloat16)
        gram_r = contract(iter_r, iter_r, 0, 0).astype(jnp.bfloat16)
        new_bl = 1.5 * iter_l.astype(jnp.float32) - 0.5 * jnp.dot(iter_l, gram_l, preferred_element_type=jnp.float32)
        new_br = 1.5 * iter_r.astype(jnp.float32) - 0.5 * jnp.dot(iter_r, gram_r, preferred_element_type=jnp.float32)
        return (new_one, new_two, new_sl, new_sr, new_bl, new_br, update)
    indices = jnp.arange(NT, dtype=jnp.int32)
    results = lax.map(tile_step, (indices, moment1, moment2, left_stats, right_stats, left_basis, right_basis))
    new_one, new_two, new_sl, new_sr, new_bl, new_br, updates = results
    update_slots = jnp.zeros((N_DP, TILE, TILE), jnp.bfloat16).at[owners[:NT]].set(updates)
    norm_total = lax.optimization_barrier(jnp.sum(norm_grads, axis=0))
    new_nm = 0.9 * norm_m + 0.1 * norm_total
    new_nv = 0.95 * norm_v + 0.05 * norm_total * norm_total
    norm_step = new_nm / FIX_ONE / (jnp.sqrt(new_nv / FIX_TWO) + 1e-08)
    norm_slots = jnp.zeros((N_DP, D), jnp.float32).at[owners[NT]].set(norm_step)
    return (new_one, new_two, new_sl, new_sr, new_bl, new_br, update_slots, new_nm, new_nv, norm_slots)
```

```python
import jax
import jax.numpy as jnp
from jax import lax
from jax.experimental import pallas as pl
from jax.experimental.pallas import tpu as pltpu
from jax.sharding import PartitionSpec as P

MESH = pl.DeviceIdType.MESH

FIX_ONE = 1.0 - 0.9**10
FIX_TWO = 1.0 - 0.95**10
BF = jnp.bfloat16
F32 = jnp.float32


def dot(left, right, left_dim, right_dim):
    return lax.dot_general(
        left, right, (((left_dim,), (right_dim,)), ((), ())), preferred_element_type=F32
    )


contract = dot


def to_tile(blocks):
    out = lax.all_to_all(blocks, "mp", split_axis=1, concat_axis=1, tiled=True)
    k, n, r, c = out.shape
    return out.transpose(0, 2, 1, 3).reshape(k, r, n * c)


def to_home(rows, n):
    k, r, c = rows.shape
    out = rows.reshape(k, r, n, c // n).transpose(0, 2, 1, 3)
    return lax.all_to_all(out, "mp", split_axis=1, concat_axis=1, tiled=True)


def gather_rows(rows):
    return lax.all_gather(rows, "dp", axis=0, tiled=True)


def normalize(power):
    wide = power.astype(F32)
    return lax.rsqrt(jnp.sum(wide * wide, axis=0, keepdims=True) + 1e-06)


def shards(
    features,
    out_grads,
    norm_grads,
    owners,
    moment1,
    moment2,
    left_stats,
    right_stats,
    left_basis,
    right_basis,
    norm_m,
    norm_v,
):
    dp = lax.axis_size("dp")
    tiles, slab, width = moment1.shape
    full = slab * dp
    me = lax.axis_index("dp")
    row0 = me * slab

    narrow = to_tile(jnp.stack([left_basis, right_basis, left_stats, right_stats]).astype(BF))
    left_full = gather_rows(narrow[0])
    right_full = gather_rows(narrow[1])

    flat = out_grads.reshape(out_grads.shape[0], tiles * width)
    partial = contract(features, flat, 0, 0).astype(BF).reshape(dp, slab, tiles * width)
    parts = lax.all_to_all(partial, "dp", split_axis=0, concat_axis=0, tiled=True)
    grad_home = jnp.sum(parts.astype(F32), axis=0).astype(BF)
    grad_home = grad_home.reshape(slab, tiles, width).transpose(1, 0, 2)
    grad_rows = to_tile(grad_home[None])[0]
    grad_full = gather_rows(grad_rows)

    wide = to_tile(jnp.stack([moment1, moment2]))

    prod_l = contract(grad_rows, grad_full, 1, 1)
    grad_cols = lax.dynamic_slice_in_dim(grad_full, row0, slab, 1)
    prod_r = contract(grad_cols, grad_full, 0, 0)
    stats_l = (0.95 * narrow[2].astype(F32) + 0.05 * prod_l).astype(BF)
    stats_r = (0.95 * narrow[3].astype(F32) + 0.05 * prod_r).astype(BF)
    power_l = contract(stats_l, left_full, 1, 0).astype(BF)
    power_r = contract(stats_r, right_full, 1, 0).astype(BF)
    power_l_full = gather_rows(power_l)
    power_r_full = gather_rows(power_r)

    left_cols = lax.dynamic_slice_in_dim(left_full, row0, slab, 1)
    half = contract(left_cols, grad_full, 0, 0).astype(BF)
    rotated = contract(half, right_full, 1, 0)
    tile_one = 0.9 * wide[0] + 0.1 * rotated
    tile_two = 0.95 * wide[1] + 0.05 * rotated * rotated
    direction = (tile_one / FIX_ONE / (jnp.sqrt(tile_two / FIX_TWO) + 1e-08)).astype(BF)
    back = contract(direction, right_full, 1, 1).astype(BF)
    back_full = gather_rows(back)

    home1 = to_home(jnp.stack([rotated, prod_l, prod_r]).astype(BF), tiles).astype(F32)
    new_one = 0.9 * moment1 + 0.1 * home1[0]
    new_two = 0.95 * moment2 + 0.05 * home1[0] * home1[0]
    new_sl = 0.95 * left_stats + 0.05 * home1[1]
    new_sr = 0.95 * right_stats + 0.05 * home1[2]

    update = contract(narrow[0], back_full, 1, 0).astype(BF)

    def refine(power_full, power_rows):
        scale = normalize(power_full)
        iter_full = (power_full.astype(F32) * scale).astype(BF)
        iter_rows = (power_rows.astype(F32) * scale).astype(BF)
        gram = contract(iter_rows, iter_full, 1, 1).astype(BF)
        return 1.5 * iter_rows.astype(F32) - 0.5 * contract(gram, iter_full, 1, 0)

    new_l = refine(power_l_full, power_l)
    new_r = refine(power_r_full, power_r)
    home2 = to_home(jnp.stack([new_l.astype(BF), new_r.astype(BF), update]), tiles)
    new_bl = home2[0].astype(F32)
    new_br = home2[1].astype(F32)
    slot_of = jnp.arange(dp, dtype=jnp.int32)[:, None, None]
    slots = jnp.zeros((dp, slab, width), BF)
    for n in range(tiles):
        slots = jnp.where(slot_of == owners[n], home2[2, n][None], slots)
    update_slot = lax.all_to_all(slots, "dp", split_axis=0, concat_axis=0, tiled=True)
    update_slot = update_slot.reshape(1, full, width)

    norm_parts = norm_grads.reshape(dp, norm_m.shape[0])
    norm_parts = lax.all_to_all(norm_parts, "dp", split_axis=0, concat_axis=0, tiled=True)
    norm_total = jnp.sum(norm_parts, axis=0)
    new_nm = 0.9 * norm_m + 0.1 * norm_total
    new_nv = 0.95 * norm_v + 0.05 * norm_total * norm_total
    norm_step = new_nm / FIX_ONE / (jnp.sqrt(new_nv / FIX_TWO) + 1e-08)
    to_owner = (jnp.arange(dp, dtype=jnp.int32) == owners[tiles])[:, None]
    norm_out = jnp.where(to_owner, norm_step[None], 0.0)
    norm_slot = lax.all_to_all(norm_out, "dp", split_axis=0, concat_axis=0, tiled=True)
    norm_slot = norm_slot.reshape(1, -1)
    return (
        new_one,
        new_two,
        new_sl,
        new_sr,
        new_bl,
        new_br,
        update_slot,
        new_nm,
        new_nv,
        norm_slot,
    )


def fused_kernel(
    feat_ref, og_ref, pack_ref, own_ref, m1_ref, m2_ref, sl_ref, sr_ref, lb_ref, rb_ref,
    rot_home, pl_home, pr_home, nl_home, nr_home, upd_out, nm_out, nv_out, ns_out,
    ft, ppart, own, xrecv, line, lsend,
    zl, zr, zsl, zsr, zm1, zm2,
    L, R, G, DIR, IL, IR, SL, SR, PL, PR, m1t, m2t, rot_s, nl_s, nr_s, upd, upd_px, sq,
    zs_send, zs_recv, x_send, x_recv, ln_send, ln_recv, ga_send, ga_recv, co_send, co_recv,
    norm_all, nscr, up_r, up_l, up_recv, ux_sem, nm_send, nm_recv, sq_send, sq_recv,
):
    nt, slab, width = m1_ref.shape
    dp = lax.axis_index("dp")
    q = lax.axis_index("mp")
    z, x = dp // 2, lax.rem(dp, 2)
    y, c = q // 2, lax.rem(q, 2)
    half = 4 * slab

    def at(zz, xx, yy, cc):
        return (zz * 2 + xx, yy * 2 + cc)

    def cols(yy, cc):
        return pl.ds(pl.multiple_of((yy * 2 + cc) * width, width), width)

    mycols = cols(y, c)

    def remote(src, dst, ssem, rsem, dev):
        return pltpu.make_async_remote_copy(
            src_ref=src, dst_ref=dst, send_sem=ssem, recv_sem=rsem, device_id=dev, device_id_type=MESH
        )

    pending = []

    def start(cp):
        cp.start()
        pending.append(cp)

    def zspread(kind, src, dst):
        for j in (1, 2, 3):
            zz = lax.rem(z + j, 4)
            start(remote(src(zz), dst(z), zs_send.at[kind, j], zs_recv.at[kind, z], at(zz, x, y, c)))

    def zwait(kind, src, dst):
        for j in (1, 2, 3):
            zz = lax.rem(z + j, 4)
            remote(src(zz), dst(zz), zs_send.at[kind, j], zs_recv.at[kind, zz], at(zz, x, y, c)).wait_recv()

    hops = ((1, 0), (0, 1), (1, 1))

    def flip(v, f):
        return 1 - v if f else v

    def gstart(kind, blk):
        own_blk = blk(x, y, c)
        for r, (fx, fy) in enumerate(hops):
            start(remote(own_blk, own_blk, ga_send.at[kind, r], ga_recv.at[kind, r], at(z, flip(x, fx), flip(y, fy), c)))
        start(remote(own_blk, own_blk, co_send.at[kind, 3], co_recv.at[kind, 3], at(z, x, y, 1 - c)))

    def gmid(kind, blk):
        for r, (fx, fy) in enumerate(hops):
            there = blk(flip(x, fx), flip(y, fy), c)
            remote(there, there, ga_send.at[kind, r], ga_recv.at[kind, r], at(z, flip(x, fx), flip(y, fy), c)).wait_recv()
            start(remote(there, there, co_send.at[kind, r], co_recv.at[kind, r], at(z, x, y, 1 - c)))

    def gend(kind, blk):
        for r, (fx, fy) in enumerate(hops + ((0, 0),)):
            there = blk(flip(x, fx), flip(y, fy), 1 - c)
            remote(there, there, co_send.at[kind, r], co_recv.at[kind, r], at(z, x, y, 1 - c)).wait_recv()

    def inter(ref):
        return lambda xx, yy, cc: ref.at[:, xx, :, cols(yy, cc)]

    def halves(ref):
        return lambda xx, yy, cc: ref.at[pl.ds(2 * xx, 2), :, :, cols(yy, cc)]

    def sstart(kind, ref):
        b = ref.at[:, :, cols(y, c)]
        start(remote(b, b, ga_send.at[kind, 0], ga_recv.at[kind, 0], at(z, x, 1 - y, c)))
        start(remote(b, b, co_send.at[kind, 0], co_recv.at[kind, 0], at(z, x, y, 1 - c)))

    def smid(kind, ref):
        b = ref.at[:, :, cols(1 - y, c)]
        remote(b, b, ga_send.at[kind, 0], ga_recv.at[kind, 0], at(z, x, 1 - y, c)).wait_recv()
        start(remote(b, b, co_send.at[kind, 1], co_recv.at[kind, 1], at(z, x, y, 1 - c)))

    def send_(kind, ref):
        for k, yy in ((0, y), (1, 1 - y)):
            b = ref.at[:, :, cols(yy, 1 - c)]
            remote(b, b, co_send.at[kind, k], co_recv.at[kind, k], at(z, x, y, 1 - c)).wait_recv()

    barrier = pltpu.get_barrier_semaphore()
    peers = [(lax.rem(dp + j, 8), q) for j in range(1, 8)]
    peers += [at(z, x, 1 - y, c), at(z, 1 - x, 1 - y, c), at(z, x, y, 1 - c)]
    for peer in peers:
        pl.semaphore_signal(barrier, inc=1, device_id=peer, device_id_type=MESH)

    zl[...] = lb_ref[...].astype(BF)
    zr[...] = rb_ref[...].astype(BF)
    L[z, x, :, mycols] = zl[z]
    R[z, x, :, mycols] = zr[z]
    norm_all[dp] = pack_ref[...]
    ft[...] = feat_ref[:, pl.ds(pl.multiple_of((1 - x) * half, half), half)].T
    pl.semaphore_wait(barrier, len(peers))

    def tile_in(src, dst):
        return (lambda zz: src.at[zz]), dst

    lz = tile_in(zl, lambda s: L.at[s, x, :, mycols])
    rz = tile_in(zr, lambda s: R.at[s, x, :, mycols])
    zspread(0, *lz)
    zspread(1, *rz)

    def tile_of(k):
        zz = jnp.minimum(z, 3 - z)
        base = (3, 2, 1 - zz, zz)[k]
        return jnp.where(z < 2, base, 3 - base)

    def og(t):
        return og_ref[:, pl.ds(pl.multiple_of(t * width, width), width)]

    for k in range(4):
        t = tile_of(k)
        ppart[t] = dot(ft[...], og(t), 1, 0).astype(BF)
        start(remote(ppart.at[t], xrecv.at[t], x_send.at[t], x_recv.at[t], at(z, 1 - x, y, c)))
    for j in range(1, 8):
        dd = lax.rem(dp + j, 8)
        start(remote(pack_ref, norm_all.at[dp], nm_send.at[j], nm_recv.at[dp], (dd, q)))
    ft[...] = feat_ref[:, pl.ds(pl.multiple_of(x * half, half), half)].T
    for k in range(4):
        t = tile_of(k)
        own[t] = dot(ft[...], og(t), 1, 0)
    zsl[...] = sl_ref[...].astype(BF)
    zsr[...] = sr_ref[...].astype(BF)
    zm1[...] = m1_ref[...].astype(BF)
    zm2[...] = m2_ref[...].astype(BF)
    SL[z, :, mycols] = zsl[z]
    SR[z, :, mycols] = zsr[z]
    m1t[z] = zm1[z]
    m2t[z] = zm2[z]

    def xwait(t):
        remote(ppart.at[t], xrecv.at[t], x_send.at[t], x_recv.at[t], at(z, 1 - x, y, c)).wait_recv()

    def lwait(d, t):
        remote(lsend.at[t], line.at[d, t], ln_send.at[t], ln_recv.at[d, t], at(z, x, y, 1 - c)).wait_recv()

    for k in range(3):
        t = tile_of(k)
        right = t > z
        d = jnp.where(right, 0, 1)
        zn = jnp.where(right, z + 1, z - 1)
        inner_hop = jnp.where(right, z > 0, z < 3)
        xwait(t)
        own[t] += xrecv[t].astype(F32)

        @pl.when(inner_hop)
        def _():
            lwait(d, t)
            lsend[t] = (own[t] + line[d, t].astype(F32)).astype(BF)

        @pl.when(jnp.logical_not(inner_hop))
        def _():
            lsend[t] = own[t].astype(BF)

        start(remote(lsend.at[t], line.at[d, t], ln_send.at[t], ln_recv.at[d, t], at(zn, x, y, c)))
        if k == 1:
            zwait(0, *lz)
            gstart(0, inter(L))
            zwait(1, *rz)
            gstart(1, inter(R))
    slz = tile_in(zsl, lambda s: SL.at[s, :, mycols])
    srz = tile_in(zsr, lambda s: SR.at[s, :, mycols])
    m1z = tile_in(zm1, lambda s: m1t.at[s])
    m2z = tile_in(zm2, lambda s: m2t.at[s])
    zspread(4, *m1z)
    zspread(5, *m2z)
    zspread(2, *slz)
    zspread(3, *srz)
    xwait(z)
    own[z] += xrecv[z].astype(F32)

    @pl.when(z > 0)
    def _():
        lwait(0, z)
        own[z] += line[0, z].astype(F32)

    @pl.when(z < 3)
    def _():
        lwait(1, z)
        own[z] += line[1, z].astype(F32)

    G[pl.ds(2 * x, 2), :, :, mycols] = own[z].astype(BF).reshape(2, 2, slab, width)
    gstart(2, halves(G))
    gmid(0, inter(L))
    gmid(1, inter(R))
    zwait(4, *m1z)
    zwait(5, *m2z)
    zwait(2, *slz)
    sstart(6, SL)
    zwait(3, *srz)
    sstart(7, SR)
    gmid(2, halves(G))
    gend(0, inter(L))
    gend(1, inter(R))
    gend(2, halves(G))

    def full(ref):
        return ref[...].reshape(8 * slab, 8 * slab)

    def rows(ref):
        return ref[:, x].reshape(half, 8 * slab)

    def colb(ref):
        return ref[:, :, :, mycols].reshape(8 * slab, width)

    def lane(ref, zz):
        return ref[:, :, :, pl.ds(pl.multiple_of((2 * zz + x) * slab, slab), slab)].reshape(8 * slab, slab)

    inner = dot(full(G), colb(R), 1, 0).astype(BF)
    for s in range(4):
        rotated = dot(lane(L, s), inner, 0, 0)
        rot_s[s] = rotated.astype(BF)
        one = 0.9 * m1t[s].astype(F32) + 0.1 * rotated
        two = 0.95 * m2t[s].astype(F32) + 0.05 * rotated * rotated
        DIR[s, x, :, mycols] = (one / FIX_ONE / (jnp.sqrt(two / FIX_TWO) + 1e-08)).astype(BF)
    gstart(3, inter(DIR))
    rot_home[z] = rot_s[z]
    rotz = tile_in(rot_s, lambda s: rot_home.at[s])
    zspread(6, *rotz)

    def power(prods, stat, basis, prod, slot):
        total = jnp.zeros((1, width), F32)
        prods[...] = prod.astype(BF)
        stats = (0.95 * stat[...].astype(F32) + 0.05 * prods[...].astype(F32)).astype(BF)
        out = dot(stats.reshape(half, 8 * slab), colb(basis), 1, 0)
        total = jnp.sum(out * out, axis=0, keepdims=True)
        sq[0, slot] = jnp.broadcast_to(total, (8, width))
        start(remote(sq.at[0, slot], sq.at[1, slot], sq_send.at[slot], sq_recv.at[slot], at(z, 1 - x, y, c)))
        return out

    def iterate(out, slot, it):
        remote(sq.at[0, slot], sq.at[1, slot], sq_send.at[slot], sq_recv.at[slot], at(z, 1 - x, y, c)).wait_recv()
        total = (sq[0, slot] + sq[1, slot])[0:1]
        it[:, x, :, mycols] = (out * lax.rsqrt(total + 1e-06)).astype(BF).reshape(4, slab, width)

    smid(6, SL)
    smid(7, SR)
    send_(6, SL)
    prod_l = dot(rows(G), full(G), 1, 1).reshape(4, slab, 8 * slab)
    pow_l = power(PL, SL, L, prod_l, 0)
    pl_home[z] = PL[z, :, mycols]
    plz = (lambda zz: PL.at[zz, :, mycols]), (lambda s: pl_home.at[s])
    zspread(7, *plz)
    send_(7, SR)
    iterate(pow_l, 0, IL)
    gstart(4, inter(IL))
    for s in range(4):
        PR[s] = dot(lane(G, s), full(G), 0, 0).astype(BF)
    pow_r = power(PR, SR, R, PR[...], 1)
    pr_home[z] = PR[z, :, mycols]
    prz = (lambda zz: PR.at[zz, :, mycols]), (lambda s: pr_home.at[s])
    zspread(8, *prz)
    iterate(pow_r, 1, IR)
    gstart(5, inter(IR))

    gmid(3, inter(DIR))
    gend(3, inter(DIR))
    back = dot(full(DIR), R[q].reshape(2 * slab, 8 * slab), 1, 1).astype(BF)
    upd[z] = dot(rows(L), back, 1, 0).astype(BF).reshape(4, slab, width)

    def ucopy(t, right):
        zn = z + 1 if right else z - 1
        zn = jnp.clip(zn, 0, 3)
        return remote(upd.at[t], upd.at[t], (up_r if right else up_l).at[t], up_recv.at[t], at(zn, x, y, c))

    @pl.when(z < 3)
    def _():
        ucopy(z, True).start()

    @pl.when(z > 0)
    def _():
        ucopy(z, False).start()

    def refine(it, kind, out_s, home, zk):
        gmid(kind, inter(it))
        gend(kind, inter(it))
        gram = dot(rows(it), full(it), 1, 1).astype(BF)
        mine = it[:, x, :, mycols].reshape(half, width).astype(F32)
        new = 1.5 * mine - 0.5 * dot(gram, colb(it), 1, 0)
        out_s[...] = new.astype(BF).reshape(4, slab, width)
        home[z] = out_s[z]
        mv = tile_in(out_s, lambda s: home.at[s])
        zspread(zk, *mv)
        return mv

    def relay(j):
        @pl.when(z - j >= 0)
        def _():
            t = jnp.maximum(z - j, 0)
            ucopy(t, True).wait_recv()

            @pl.when(z < 3)
            def _():
                ucopy(t, True).start()

        @pl.when(z + j <= 3)
        def _():
            t = jnp.minimum(z + j, 3)
            ucopy(t, False).wait_recv()

            @pl.when(z > 0)
            def _():
                ucopy(t, False).start()

    nlz = refine(IL, 4, nl_s, nl_home, 9)
    relay(1)
    nrz = refine(IR, 5, nr_s, nr_home, 10)
    relay(2)
    relay(3)

    def pick(who):
        got = jnp.zeros((4, slab, width), BF)
        for t in range(4):
            got = jnp.where(own_ref[t] == who, upd[t], got)
        return got

    upd_px[...] = pick(z * 2 + 1 - x)
    ux = remote(upd_px, upd_out.at[:, x], ux_sem.at[0], ux_sem.at[1], at(z, 1 - x, y, c))
    ux.start()
    upd_out[:, x] = pick(dp)
    for j in range(1, 8):
        dd = lax.rem(dp + j, 8)
        remote(pack_ref, norm_all.at[dd], nm_send.at[j], nm_recv.at[dd], (dd, q)).wait_recv()
    for j in range(8):
        nscr[0, 2 * j : 2 * j + 2] = norm_all[j, 16:18]
        nscr[1, 2 * j : 2 * j + 2] = norm_all[j, 18:20]
    total = jnp.sum(norm_all[:, 0:16], axis=0)
    nm = 0.9 * nscr[0] + 0.1 * total
    nv = 0.95 * nscr[1] + 0.05 * total * total
    step = nm / FIX_ONE / (jnp.sqrt(nv / FIX_TWO) + 1e-08)
    ns_out[...] = jnp.where(own_ref[nt] == dp, step, jnp.zeros_like(step))
    nscr[0] = nm
    nscr[1] = nv
    nm_out[...] = nscr[0, pl.ds(2 * dp, 2)]
    nv_out[...] = nscr[1, pl.ds(2 * dp, 2)]
    zwait(6, *rotz)
    zwait(7, *plz)
    zwait(8, *prz)
    zwait(9, *nlz)
    zwait(10, *nrz)
    ux.wait_send()
    remote(upd_px, upd_out.at[:, 1 - x], ux_sem.at[0], ux_sem.at[1], at(z, 1 - x, y, c)).wait_recv()

    @pl.when(z < 3)
    def _():
        for j in range(4):
            @pl.when(z - j >= 0)
            def _():
                ucopy(jnp.maximum(z - j, 0), True).wait_send()

    @pl.when(z > 0)
    def _():
        for j in range(4):
            @pl.when(z + j <= 3)
            def _():
                ucopy(jnp.minimum(z + j, 3), False).wait_send()

    for cp in pending:
        cp.wait_send()


def fused_shards(
    features,
    out_grads,
    norm_grads,
    owners,
    moment1,
    moment2,
    left_stats,
    right_stats,
    left_basis,
    right_basis,
    norm_m,
    norm_v,
):
    nt, slab, width = moment1.shape
    full = 8 * slab
    flat = out_grads.reshape(out_grads.shape[0], nt * width)
    pack = jnp.concatenate(
        [norm_grads.reshape(16, 128), norm_m.reshape(2, 128), norm_v.reshape(2, 128), jnp.zeros((4, 128), F32)]
    )
    vm = pl.BlockSpec(memory_space=pltpu.VMEM)
    home = jax.ShapeDtypeStruct((nt, slab, width), BF)
    big = pltpu.VMEM((4, 2, slab, full), BF)
    blk = pltpu.VMEM((4, slab, width), BF)
    piece = (4 * slab, width)
    dma = pltpu.SemaphoreType.DMA
    rot, prod_l, prod_r, new_l, new_r, slot, nm, nv, ns = pl.pallas_call(
        fused_kernel,
        out_shape=[home] * 5
        + [
            jax.ShapeDtypeStruct((4, 2, slab, width), BF),
            jax.ShapeDtypeStruct((2, 128), F32),
            jax.ShapeDtypeStruct((2, 128), F32),
            jax.ShapeDtypeStruct((16, 128), F32),
        ],
        in_specs=[vm] * 3 + [pl.BlockSpec(memory_space=pltpu.SMEM)] + [vm] * 6,
        out_specs=[vm] * 9,
        scratch_shapes=[
            pltpu.VMEM((4 * slab, features.shape[0]), BF),
            pltpu.VMEM((4,) + piece, BF),
            pltpu.VMEM((4,) + piece, F32),
            pltpu.VMEM((4,) + piece, BF),
            pltpu.VMEM((2, 4) + piece, BF),
            pltpu.VMEM((4,) + piece, BF),
        ]
        + [blk] * 6
        + [big] * 6
        + [pltpu.VMEM((4, slab, full), BF)] * 4
        + [blk] * 5
        + [pltpu.VMEM((4, 4, slab, width), BF), blk, pltpu.VMEM((2, 2, 8, width), F32)]
        + [
            dma((11, 4)), dma((11, 4)), dma((4,)), dma((4,)), dma((4,)), dma((2, 4)),
            dma((8, 3)), dma((8, 3)), dma((8, 4)), dma((8, 4)),
        ]
        + [pltpu.VMEM((8, 24, 128), F32), pltpu.VMEM((2, 16, 128), F32)]
        + [dma((4,)), dma((4,)), dma((4,)), dma((2,)), dma((8,)), dma((8,)), dma((2,)), dma((2,))],
        compiler_params=pltpu.CompilerParams(
            collective_id=0, has_side_effects=True, vmem_limit_bytes=56 * 2**20
        ),
        cost_estimate=pl.CostEstimate(flops=10**10, bytes_accessed=2**24, transcendentals=0),
    )(features, flat, pack, owners, moment1, moment2, left_stats, right_stats, left_basis, right_basis)
    rot, prod_l, prod_r = rot.astype(F32), prod_l.astype(F32), prod_r.astype(F32)
    return (
        0.9 * moment1 + 0.1 * rot,
        0.95 * moment2 + 0.05 * rot * rot,
        0.95 * left_stats + 0.05 * prod_l,
        0.95 * right_stats + 0.05 * prod_r,
        new_l.astype(F32),
        new_r.astype(F32),
        slot.reshape(1, full, width),
        nm.reshape(norm_m.shape),
        nv.reshape(norm_v.shape),
        ns.reshape(1, -1),
    )


def solution(mesh):
    in_specs = (
        P("dp", None),
        P("dp", None, "mp"),
        P("dp", None),
        P(),
        P(None, "dp", "mp"),
        P(None, "dp", "mp"),
        P(None, "dp", "mp"),
        P(None, "dp", "mp"),
        P(None, "dp", "mp"),
        P(None, "dp", "mp"),
        P("dp"),
        P("dp"),
    )
    out_specs = (
        P(None, "dp", "mp"),
        P(None, "dp", "mp"),
        P(None, "dp", "mp"),
        P(None, "dp", "mp"),
        P(None, "dp", "mp"),
        P(None, "dp", "mp"),
        P("dp", None, "mp"),
        P("dp"),
        P("dp"),
        P("dp", None),
    )
    fused = mesh.shape["dp"] == 8 and mesh.shape["mp"] == 4
    body = fused_shards if fused else shards
    return jax.shard_map(body, mesh=mesh, in_specs=in_specs, out_specs=out_specs, check_vma=False)
```

```python
import jax
import jax.numpy as jnp
from jax import lax
from jax.experimental import pallas as pl
from jax.experimental.pallas import tpu as pltpu
from jax.sharding import PartitionSpec as P

MESH = pl.DeviceIdType.MESH

FIX_ONE = 1.0 - 0.9**10
FIX_TWO = 1.0 - 0.95**10
BF = jnp.bfloat16
F32 = jnp.float32


def dot(left, right, left_dim, right_dim):
    return lax.dot_general(
        left, right, (((left_dim,), (right_dim,)), ((), ())), preferred_element_type=F32
    )


contract = dot


def to_tile(blocks):
    out = lax.all_to_all(blocks, "mp", split_axis=1, concat_axis=1, tiled=True)
    k, n, r, c = out.shape
    return out.transpose(0, 2, 1, 3).reshape(k, r, n * c)


def to_home(rows, n):
    k, r, c = rows.shape
    out = rows.reshape(k, r, n, c // n).transpose(0, 2, 1, 3)
    return lax.all_to_all(out, "mp", split_axis=1, concat_axis=1, tiled=True)


def gather_rows(rows):
    return lax.all_gather(rows, "dp", axis=0, tiled=True)


def normalize(power):
    wide = power.astype(F32)
    return lax.rsqrt(jnp.sum(wide * wide, axis=0, keepdims=True) + 1e-06)


def shards(
    features,
    out_grads,
    norm_grads,
    owners,
    moment1,
    moment2,
    left_stats,
    right_stats,
    left_basis,
    right_basis,
    norm_m,
    norm_v,
):
    dp = lax.axis_size("dp")
    tiles, slab, width = moment1.shape
    full = slab * dp
    me = lax.axis_index("dp")
    row0 = me * slab

    narrow = to_tile(jnp.stack([left_basis, right_basis, left_stats, right_stats]).astype(BF))
    left_full = gather_rows(narrow[0])
    right_full = gather_rows(narrow[1])

    flat = out_grads.reshape(out_grads.shape[0], tiles * width)
    partial = contract(features, flat, 0, 0).astype(BF).reshape(dp, slab, tiles * width)
    parts = lax.all_to_all(partial, "dp", split_axis=0, concat_axis=0, tiled=True)
    grad_home = jnp.sum(parts.astype(F32), axis=0).astype(BF)
    grad_home = grad_home.reshape(slab, tiles, width).transpose(1, 0, 2)
    grad_rows = to_tile(grad_home[None])[0]
    grad_full = gather_rows(grad_rows)

    wide = to_tile(jnp.stack([moment1, moment2]))

    prod_l = contract(grad_rows, grad_full, 1, 1)
    grad_cols = lax.dynamic_slice_in_dim(grad_full, row0, slab, 1)
    prod_r = contract(grad_cols, grad_full, 0, 0)
    stats_l = (0.95 * narrow[2].astype(F32) + 0.05 * prod_l).astype(BF)
    stats_r = (0.95 * narrow[3].astype(F32) + 0.05 * prod_r).astype(BF)
    power_l = contract(stats_l, left_full, 1, 0).astype(BF)
    power_r = contract(stats_r, right_full, 1, 0).astype(BF)
    power_l_full = gather_rows(power_l)
    power_r_full = gather_rows(power_r)

    left_cols = lax.dynamic_slice_in_dim(left_full, row0, slab, 1)
    half = contract(left_cols, grad_full, 0, 0).astype(BF)
    rotated = contract(half, right_full, 1, 0)
    tile_one = 0.9 * wide[0] + 0.1 * rotated
    tile_two = 0.95 * wide[1] + 0.05 * rotated * rotated
    direction = (tile_one / FIX_ONE / (jnp.sqrt(tile_two / FIX_TWO) + 1e-08)).astype(BF)
    back = contract(direction, right_full, 1, 1).astype(BF)
    back_full = gather_rows(back)

    home1 = to_home(jnp.stack([rotated, prod_l, prod_r]).astype(BF), tiles).astype(F32)
    new_one = 0.9 * moment1 + 0.1 * home1[0]
    new_two = 0.95 * moment2 + 0.05 * home1[0] * home1[0]
    new_sl = 0.95 * left_stats + 0.05 * home1[1]
    new_sr = 0.95 * right_stats + 0.05 * home1[2]

    update = contract(narrow[0], back_full, 1, 0).astype(BF)

    def refine(power_full, power_rows):
        scale = normalize(power_full)
        iter_full = (power_full.astype(F32) * scale).astype(BF)
        iter_rows = (power_rows.astype(F32) * scale).astype(BF)
        gram = contract(iter_rows, iter_full, 1, 1).astype(BF)
        return 1.5 * iter_rows.astype(F32) - 0.5 * contract(gram, iter_full, 1, 0)

    new_l = refine(power_l_full, power_l)
    new_r = refine(power_r_full, power_r)
    home2 = to_home(jnp.stack([new_l.astype(BF), new_r.astype(BF), update]), tiles)
    new_bl = home2[0].astype(F32)
    new_br = home2[1].astype(F32)
    slot_of = jnp.arange(dp, dtype=jnp.int32)[:, None, None]
    slots = jnp.zeros((dp, slab, width), BF)
    for n in range(tiles):
        slots = jnp.where(slot_of == owners[n], home2[2, n][None], slots)
    update_slot = lax.all_to_all(slots, "dp", split_axis=0, concat_axis=0, tiled=True)
    update_slot = update_slot.reshape(1, full, width)

    norm_parts = norm_grads.reshape(dp, norm_m.shape[0])
    norm_parts = lax.all_to_all(norm_parts, "dp", split_axis=0, concat_axis=0, tiled=True)
    norm_total = jnp.sum(norm_parts, axis=0)
    new_nm = 0.9 * norm_m + 0.1 * norm_total
    new_nv = 0.95 * norm_v + 0.05 * norm_total * norm_total
    norm_step = new_nm / FIX_ONE / (jnp.sqrt(new_nv / FIX_TWO) + 1e-08)
    to_owner = (jnp.arange(dp, dtype=jnp.int32) == owners[tiles])[:, None]
    norm_out = jnp.where(to_owner, norm_step[None], 0.0)
    norm_slot = lax.all_to_all(norm_out, "dp", split_axis=0, concat_axis=0, tiled=True)
    norm_slot = norm_slot.reshape(1, -1)
    return (
        new_one,
        new_two,
        new_sl,
        new_sr,
        new_bl,
        new_br,
        update_slot,
        new_nm,
        new_nv,
        norm_slot,
    )


def fused_kernel(
    feat_hbm, og_hbm, ng_ref, nmi_ref, nvi_ref, own_ref, m1_hbm, m2_hbm, sl_hbm, sr_hbm, lb_hbm, rb_hbm,
    rot_home, pl_home, pr_home, nl_home, nr_home, upd_out, nm_out, nv_out, ns_out,
    feat_ref, og_ref, m1_ref, m2_ref, sl_ref, sr_ref, lb_ref, rb_ref, pack_ref, in_sem,
    ft, ppart, own, xrecv, line, lsend,
    zl, zr, zsl, zsr, zm1, zm2,
    L, R, G, DIR, IL, IR, SL, SR, PL, PR, m1t, m2t, rot_s, nl_s, nr_s, upd, upd_px, sq,
    zs_send, zs_recv, x_send, x_recv, ln_send, ln_recv, ga_send, ga_recv, co_send, co_recv,
    norm_all, nscr, up_r, up_l, up_recv, ux_sem, nm_send, nm_recv, sq_send, sq_recv,
):
    nt, slab, width = m1_ref.shape
    dp = lax.axis_index("dp")
    q = lax.axis_index("mp")
    z, x = dp // 2, lax.rem(dp, 2)
    y, c = q // 2, lax.rem(q, 2)
    half = 4 * slab

    def at(zz, xx, yy, cc):
        return (zz * 2 + xx, yy * 2 + cc)

    def cols(yy, cc):
        return pl.ds(pl.multiple_of((yy * 2 + cc) * width, width), width)

    mycols = cols(y, c)

    def remote(src, dst, ssem, rsem, dev):
        return pltpu.make_async_remote_copy(
            src_ref=src, dst_ref=dst, send_sem=ssem, recv_sem=rsem, device_id=dev, device_id_type=MESH
        )

    pending = []

    def start(cp):
        cp.start()
        pending.append(cp)

    def zspread(kind, src, dst):
        for j in (1, 2, 3):
            zz = lax.rem(z + j, 4)
            start(remote(src(zz), dst(z), zs_send.at[kind, j], zs_recv.at[kind, z], at(zz, x, y, c)))

    def zwait(kind, src, dst):
        for j in (1, 2, 3):
            zz = lax.rem(z + j, 4)
            remote(src(zz), dst(zz), zs_send.at[kind, j], zs_recv.at[kind, zz], at(zz, x, y, c)).wait_recv()

    xdev, ydev, cdev = at(z, 1 - x, y, c), at(z, x, 1 - y, c), at(z, x, y, 1 - c)

    def ga(kind, slot, ref, dev):
        return remote(ref, ref, ga_send.at[kind, slot], ga_recv.at[kind, slot], dev)

    def co(kind, slot, ref):
        return remote(ref, ref, co_send.at[kind, slot], co_recv.at[kind, slot], cdev)

    def gstart(kind, blk):
        b = blk(x, y, c, 0, 4)
        start(ga(kind, 0, b, xdev))
        start(ga(kind, 1, b, ydev))
        start(co(kind, 0, b))

    def gmid(kind, blk):
        ga(kind, 0, blk(1 - x, y, c, 0, 4), xdev).wait_recv()
        start(ga(kind, 2, blk(1 - x, y, c, 0, 2), ydev))
        start(co(kind, 1, blk(1 - x, y, c, 0, 4)))
        ga(kind, 1, blk(x, 1 - y, c, 0, 4), ydev).wait_recv()
        start(ga(kind, 3, blk(x, 1 - y, c, 2, 4), xdev))
        start(co(kind, 2, blk(x, 1 - y, c, 0, 4)))

    def gend(kind, blk):
        ga(kind, 2, blk(1 - x, 1 - y, c, 0, 2), ydev).wait_recv()
        start(co(kind, 3, blk(1 - x, 1 - y, c, 0, 2)))
        ga(kind, 3, blk(1 - x, 1 - y, c, 2, 4), xdev).wait_recv()
        start(co(kind, 4, blk(1 - x, 1 - y, c, 2, 4)))
        co(kind, 0, blk(x, y, 1 - c, 0, 4)).wait_recv()
        co(kind, 1, blk(1 - x, y, 1 - c, 0, 4)).wait_recv()
        co(kind, 2, blk(x, 1 - y, 1 - c, 0, 4)).wait_recv()
        co(kind, 3, blk(1 - x, 1 - y, 1 - c, 0, 2)).wait_recv()
        co(kind, 4, blk(1 - x, 1 - y, 1 - c, 2, 4)).wait_recv()

    def inter(ref):
        return lambda xx, yy, cc, a, b: ref.at[pl.ds(a, b - a), xx, :, cols(yy, cc)]

    def halves(ref):
        def blk(xx, yy, cc, a, b):
            if b - a == 4:
                return ref.at[pl.ds(2 * xx, 2), :, :, cols(yy, cc)]
            return ref.at[2 * xx + a // 2, :, :, cols(yy, cc)]

        return blk

    def bstart(kind, ref, part):
        start(ga(kind, 0, ref.at[:, x, :, mycols], xdev))
        start(ga(kind, 1, part(ref, 1 - y, x, y, c), ydev))
        start(co(kind, 0, part(ref, y, x, y, c)))

    def bx(kind, ref, part):
        ga(kind, 0, ref.at[:, 1 - x, :, mycols], xdev).wait_recv()
        start(ga(kind, 2, part(ref, 1 - y, 1 - x, y, c), ydev))
        start(co(kind, 1, part(ref, y, 1 - x, y, c)))

    def bc(kind, ref, part):
        ga(kind, 1, part(ref, y, x, 1 - y, c), ydev).wait_recv()
        start(co(kind, 2, part(ref, y, x, 1 - y, c)))
        ga(kind, 2, part(ref, y, 1 - x, 1 - y, c), ydev).wait_recv()
        start(co(kind, 3, part(ref, y, 1 - x, 1 - y, c)))

    def bend(kind, ref, part):
        for n, (xx, yy) in enumerate(((x, y), (1 - x, y), (x, 1 - y), (1 - x, 1 - y))):
            co(kind, n, part(ref, y, xx, yy, 1 - c)).wait_recv()

    def allrows(ref, to_y, xx, yy, cc):
        return ref.at[:, xx, :, cols(yy, cc)]

    def tworows(ref, to_y, xx, yy, cc):
        return ref.at[pl.ds(2 * to_y, 2), xx, :, cols(yy, cc)]

    def rstart(kind, rowref):
        b = rowref(y, c)
        start(ga(kind, 0, b, ydev))
        start(co(kind, 0, b))

    def rmid(kind, rowref):
        ga(kind, 0, rowref(1 - y, c), ydev).wait_recv()
        start(co(kind, 1, rowref(1 - y, c)))

    def rend(kind, rowref):
        co(kind, 0, rowref(y, 1 - c)).wait_recv()
        co(kind, 1, rowref(1 - y, 1 - c)).wait_recv()

    def srows(ref):
        return lambda yy, cc: ref.at[:, :, cols(yy, cc)]

    def xrows(ref):
        return lambda yy, cc: ref.at[:, x, :, cols(yy, cc)]

    barrier = pltpu.get_barrier_semaphore()
    peers = [(lax.rem(dp + j, 8), q) for j in range(1, 8)]
    peers += [at(z, x, 1 - y, c), at(z, 1 - x, 1 - y, c), at(z, x, y, 1 - c)]
    for peer in peers:
        pl.semaphore_signal(barrier, inc=1, device_id=peer, device_id_type=MESH)

    loads = {}
    for n, (src, dst) in enumerate((
        (feat_hbm, feat_ref), (og_hbm, og_ref), (lb_hbm, lb_ref), (rb_hbm, rb_ref),
        (m1_hbm, m1_ref), (m2_hbm, m2_ref), (sl_hbm, sl_ref), (sr_hbm, sr_ref),
    )):
        loads[n] = pltpu.make_async_copy(src, dst, in_sem.at[n])
        loads[n].start()
    pack_ref[0:16] = ng_ref[...]
    pack_ref[16:18] = nmi_ref[...]
    pack_ref[18:20] = nvi_ref[...]
    pack_ref[20:24] = jnp.zeros((4, 128), F32)
    norm_all[dp] = pack_ref[...]
    loads[0].wait()
    ft[...] = feat_ref[:, pl.ds(pl.multiple_of((1 - x) * half, half), half)].T
    loads[1].wait()

    def tile_of(k):
        zz = jnp.minimum(z, 3 - z)
        base = (3, 2, 1 - zz, zz)[k]
        return jnp.where(z < 2, base, 3 - base)

    def og(t):
        return og_ref[:, pl.ds(pl.multiple_of(t * width, width), width)]

    def partial(k):
        t = tile_of(k)
        ppart[t] = dot(ft[...], og(t), 1, 0).astype(BF)

    def xsend(k):
        t = tile_of(k)
        start(remote(ppart.at[t], xrecv.at[t], x_send.at[t], x_recv.at[t], xdev))

    partial(0)
    loads[2].wait()
    loads[3].wait()
    zl[...] = lb_ref[...].astype(BF)
    zr[...] = rb_ref[...].astype(BF)
    L[z, x, :, mycols] = zl[z]
    R[z, x, :, mycols] = zr[z]
    pl.semaphore_wait(barrier, len(peers))

    def tile_in(src, dst):
        return (lambda zz: src.at[zz]), dst

    lz = tile_in(zl, lambda s: L.at[s, x, :, mycols])
    rz = tile_in(zr, lambda s: R.at[s, x, :, mycols])
    xsend(0)
    zspread(0, *lz)
    zspread(1, *rz)
    partial(1)
    xsend(1)
    partial(2)
    partial(3)
    for j in range(1, 8):
        dd = lax.rem(dp + j, 8)
        start(remote(pack_ref, norm_all.at[dp], nm_send.at[j], nm_recv.at[dp], (dd, q)))
    ft[...] = feat_ref[:, pl.ds(pl.multiple_of(x * half, half), half)].T
    for k in range(4):
        t = tile_of(k)
        own[t] = dot(ft[...], og(t), 1, 0)
    for n in range(4, 8):
        loads[n].wait()
    zsl[...] = sl_ref[...].astype(BF)
    zsr[...] = sr_ref[...].astype(BF)
    zm1[...] = m1_ref[...].astype(BF)
    zm2[...] = m2_ref[...].astype(BF)
    SL[z, :, mycols] = zsl[z]
    SR[z, :, mycols] = zsr[z]
    m1t[z] = zm1[z]
    m2t[z] = zm2[z]

    def xwait(t):
        remote(ppart.at[t], xrecv.at[t], x_send.at[t], x_recv.at[t], at(z, 1 - x, y, c)).wait_recv()

    def lwait(d, t):
        remote(lsend.at[t], line.at[d, t], ln_send.at[t], ln_recv.at[d, t], at(z, x, y, 1 - c)).wait_recv()

    slz = tile_in(zsl, lambda s: SL.at[s, :, mycols])
    srz = tile_in(zsr, lambda s: SR.at[s, :, mycols])
    m1z = tile_in(zm1, lambda s: m1t.at[s])
    m2z = tile_in(zm2, lambda s: m2t.at[s])

    def hop(k):
        t = tile_of(k)
        right = t > z
        d = jnp.where(right, 0, 1)
        zn = jnp.where(right, z + 1, z - 1)
        inner_hop = jnp.where(right, z > 0, z < 3)
        xwait(t)
        own[t] += xrecv[t].astype(F32)

        @pl.when(inner_hop)
        def _():
            lwait(d, t)
            lsend[t] = (own[t] + line[d, t].astype(F32)).astype(BF)

        @pl.when(jnp.logical_not(inner_hop))
        def _():
            lsend[t] = own[t].astype(BF)

        start(remote(lsend.at[t], line.at[d, t], ln_send.at[t], ln_recv.at[d, t], at(zn, x, y, c)))

    zwait(0, *lz)
    bstart(0, L, allrows)
    xsend(2)
    hop(0)
    zspread(2, *slz)
    zwait(1, *rz)
    bstart(1, R, tworows)
    xsend(3)
    hop(1)
    zspread(3, *srz)
    bx(0, L, allrows)
    hop(2)
    zspread(4, *m1z)
    zspread(5, *m2z)
    bx(1, R, tworows)
    zwait(2, *slz)
    rstart(6, srows(SL))
    bc(0, L, allrows)
    xwait(z)
    own[z] += xrecv[z].astype(F32)

    @pl.when(z > 0)
    def _():
        lwait(0, z)
        own[z] += line[0, z].astype(F32)

    @pl.when(z < 3)
    def _():
        lwait(1, z)
        own[z] += line[1, z].astype(F32)

    G[pl.ds(2 * x, 2), :, :, mycols] = own[z].astype(BF).reshape(2, 2, slab, width)
    gstart(2, halves(G))
    gmid(2, halves(G))
    zwait(3, *srz)
    rstart(7, srows(SR))
    bc(1, R, tworows)
    bend(0, L, allrows)
    bend(1, R, tworows)
    gend(2, halves(G))
    zwait(4, *m1z)
    zwait(5, *m2z)

    def full(ref):
        return ref[...].reshape(8 * slab, 8 * slab)

    def rows(ref):
        return ref[:, x].reshape(half, 8 * slab)

    def colb(ref):
        return ref[:, :, :, mycols].reshape(8 * slab, width)

    def lane(ref, zz):
        return ref[:, :, :, pl.ds(pl.multiple_of((2 * zz + x) * slab, slab), slab)].reshape(8 * slab, slab)

    inner = dot(full(G), colb(R), 1, 0).astype(BF)
    for s in range(4):
        rotated = dot(lane(L, s), inner, 0, 0)
        rot_s[s] = rotated.astype(BF)
        one = 0.9 * m1t[s].astype(F32) + 0.1 * rotated
        two = 0.95 * m2t[s].astype(F32) + 0.05 * rotated * rotated
        DIR[s, x, :, mycols] = (one / FIX_ONE / (jnp.sqrt(two / FIX_TWO) + 1e-08)).astype(BF)
    gstart(3, inter(DIR))
    rot_home[z] = rot_s[z]
    rotz = tile_in(rot_s, lambda s: rot_home.at[s])
    zspread(6, *rotz)

    def power(prods, stat, basis, prod, slot):
        prods[...] = prod.astype(BF)
        stats = (0.95 * stat[...].astype(F32) + 0.05 * prods[...].astype(F32)).astype(BF)
        out = dot(stats.reshape(half, 8 * slab), colb(basis), 1, 0)
        total = jnp.sum(out * out, axis=0, keepdims=True)
        sq[0, slot] = jnp.broadcast_to(total, (8, width))
        start(remote(sq.at[0, slot], sq.at[1, slot], sq_send.at[slot], sq_recv.at[slot], at(z, 1 - x, y, c)))
        return out

    def iterate(out, slot, it):
        remote(sq.at[0, slot], sq.at[1, slot], sq_send.at[slot], sq_recv.at[slot], at(z, 1 - x, y, c)).wait_recv()
        total = (sq[0, slot] + sq[1, slot])[0:1]
        it[:, x, :, mycols] = (out * lax.rsqrt(total + 1e-06)).astype(BF).reshape(4, slab, width)

    rmid(6, srows(SL))
    prod_l = dot(rows(G), full(G), 1, 1).reshape(4, slab, 8 * slab)
    rend(6, srows(SL))
    pow_l = power(PL, SL, L, prod_l, 0)
    pl_home[z] = PL[z, :, mycols]
    plz = (lambda zz: PL.at[zz, :, mycols]), (lambda s: pl_home.at[s])
    zspread(7, *plz)
    rmid(7, srows(SR))
    for s in range(4):
        PR[s] = dot(lane(G, s), full(G), 0, 0).astype(BF)
    rend(7, srows(SR))
    pow_r = power(PR, SR, R, PR[...], 1)
    pr_home[z] = PR[z, :, mycols]
    prz = (lambda zz: PR.at[zz, :, mycols]), (lambda s: pr_home.at[s])
    iterate(pow_l, 0, IL)
    gmid(3, inter(DIR))
    gstart(4, inter(IL))
    iterate(pow_r, 1, IR)
    gstart(5, inter(IR))

    gend(3, inter(DIR))
    back = dot(full(DIR), R[q].reshape(2 * slab, 8 * slab), 1, 1).astype(BF)
    upd[z] = dot(rows(L), back, 1, 0).astype(BF).reshape(4, slab, width)

    def ucopy(t, h, right):
        zn = jnp.clip(z + 1 if right else z - 1, 0, 3)
        part = upd.at[t, pl.ds(2 * h, 2)]
        return remote(part, part, (up_r if right else up_l).at[t, h], up_recv.at[t, h], at(zn, x, y, c))

    def upd_on(t, h, right):
        @pl.when(z < 3 if right else z > 0)
        def _():
            ucopy(t, h, right).start()

    for h in range(2):
        upd_on(z, h, True)
        upd_on(z, h, False)
    zspread(8, *prz)
    gmid(4, inter(IL))

    def refine(it, kind, out_s, home, zk):
        gend(kind, inter(it))
        gram = dot(rows(it), full(it), 1, 1).astype(BF)
        mine = it[:, x, :, mycols].reshape(half, width).astype(F32)
        new = 1.5 * mine - 0.5 * dot(gram, colb(it), 1, 0)
        out_s[...] = new.astype(BF).reshape(4, slab, width)
        home[z] = out_s[z]
        mv = tile_in(out_s, lambda s: home.at[s])
        zspread(zk, *mv)
        return mv

    def relay(j, h):
        @pl.when(z - j >= 0)
        def _():
            t = jnp.maximum(z - j, 0)
            ucopy(t, h, True).wait_recv()
            upd_on(t, h, True)

        @pl.when(z + j <= 3)
        def _():
            t = jnp.minimum(z + j, 3)
            ucopy(t, h, False).wait_recv()
            upd_on(t, h, False)

    gmid(5, inter(IR))
    relay(1, 0)
    relay(1, 1)
    nlz = refine(IL, 4, nl_s, nl_home, 9)
    relay(2, 0)
    relay(2, 1)
    nrz = refine(IR, 5, nr_s, nr_home, 10)

    def pick(who, h):
        got = jnp.zeros((2, slab, width), BF)
        for t in range(4):
            got = jnp.where(own_ref[t] == who, upd[t, 2 * h : 2 * h + 2], got)
        return got

    def ucross(h, to):
        return remote(
            upd_px.at[2 * h : 2 * h + 2], upd_out.at[2 * h : 2 * h + 2, to], ux_sem.at[h], ux_sem.at[2 + h], xdev
        )

    for h in range(2):
        relay(3, h)
        upd_px[2 * h : 2 * h + 2] = pick(z * 2 + 1 - x, h)
        start(ucross(h, x))
        upd_out[2 * h : 2 * h + 2, x] = pick(dp, h)
    for j in range(1, 8):
        dd = lax.rem(dp + j, 8)
        remote(pack_ref, norm_all.at[dd], nm_send.at[j], nm_recv.at[dd], (dd, q)).wait_recv()
    for j in range(8):
        nscr[0, 2 * j : 2 * j + 2] = norm_all[j, 16:18]
        nscr[1, 2 * j : 2 * j + 2] = norm_all[j, 18:20]
    total = jnp.sum(norm_all[:, 0:16], axis=0)
    nm = 0.9 * nscr[0] + 0.1 * total
    nv = 0.95 * nscr[1] + 0.05 * total * total
    step = nm / FIX_ONE / (jnp.sqrt(nv / FIX_TWO) + 1e-08)
    ns_out[...] = jnp.where(own_ref[nt] == dp, step, jnp.zeros_like(step))
    nscr[0] = nm
    nscr[1] = nv
    nm_out[...] = nscr[0, pl.ds(2 * dp, 2)]
    nv_out[...] = nscr[1, pl.ds(2 * dp, 2)]
    zwait(6, *rotz)
    zwait(7, *plz)
    zwait(8, *prz)
    zwait(9, *nlz)
    zwait(10, *nrz)
    for h in range(2):
        ucross(h, 1 - x).wait_recv()

    @pl.when(z < 3)
    def _():
        for j in range(4):
            @pl.when(z - j >= 0)
            def _():
                for h in range(2):
                    ucopy(jnp.maximum(z - j, 0), h, True).wait_send()

    @pl.when(z > 0)
    def _():
        for j in range(4):
            @pl.when(z + j <= 3)
            def _():
                for h in range(2):
                    ucopy(jnp.minimum(z + j, 3), h, False).wait_send()

    for cp in pending:
        cp.wait_send()


def finish_kernel(
    m1, m2, sl, sr, rot, prod_l, prod_r, new_l, new_r, slot, nm, nv, ns,
    m1_out, m2_out, sl_out, sr_out, bl_out, br_out, slot_out, nm_out, nv_out, ns_out,
):
    turned = rot[...].astype(F32)
    m1_out[...] = 0.9 * m1[...] + 0.1 * turned
    m2_out[...] = 0.95 * m2[...] + 0.05 * turned * turned
    sl_out[...] = 0.95 * sl[...] + 0.05 * prod_l[...].astype(F32)
    sr_out[...] = 0.95 * sr[...] + 0.05 * prod_r[...].astype(F32)
    bl_out[...] = new_l[...].astype(F32)
    br_out[...] = new_r[...].astype(F32)
    slot_out[...] = slot[...]
    nm_out[...] = nm[...]
    nv_out[...] = nv[...]
    ns_out[...] = ns[...]


def fused_shards(
    features,
    out_grads,
    norm_grads,
    owners,
    moment1,
    moment2,
    left_stats,
    right_stats,
    left_basis,
    right_basis,
    norm_m,
    norm_v,
):
    nt, slab, width = moment1.shape
    full = 8 * slab
    flat = out_grads.reshape(out_grads.shape[0], nt * width)
    vm = pl.BlockSpec(memory_space=pltpu.VMEM)
    hbm = pl.BlockSpec(memory_space=pl.ANY)
    home = jax.ShapeDtypeStruct((nt, slab, width), BF)
    big = pltpu.VMEM((4, 2, slab, full), BF)
    blk = pltpu.VMEM((4, slab, width), BF)
    piece = (4 * slab, width)
    dma = pltpu.SemaphoreType.DMA
    rot, prod_l, prod_r, new_l, new_r, slot, nm, nv, ns = pl.pallas_call(
        fused_kernel,
        out_shape=[home] * 5
        + [
            jax.ShapeDtypeStruct((4, 2, slab, width), BF),
            jax.ShapeDtypeStruct((2, 128), F32),
            jax.ShapeDtypeStruct((2, 128), F32),
            jax.ShapeDtypeStruct((16, 128), F32),
        ],
        in_specs=[hbm] * 2 + [vm] * 3 + [pl.BlockSpec(memory_space=pltpu.SMEM)] + [hbm] * 6,
        out_specs=[vm] * 9,
        scratch_shapes=[
            pltpu.VMEM(features.shape, BF),
            pltpu.VMEM(flat.shape, BF),
        ]
        + [pltpu.VMEM((nt, slab, width), F32)] * 6
        + [pltpu.VMEM((24, 128), F32), dma((8,))]
        + [
            pltpu.VMEM((4 * slab, features.shape[0]), BF),
            pltpu.VMEM((4,) + piece, BF),
            pltpu.VMEM((4,) + piece, F32),
            pltpu.VMEM((4,) + piece, BF),
            pltpu.VMEM((2, 4) + piece, BF),
            pltpu.VMEM((4,) + piece, BF),
        ]
        + [blk] * 6
        + [big] * 6
        + [pltpu.VMEM((4, slab, full), BF)] * 4
        + [blk] * 5
        + [pltpu.VMEM((4, 4, slab, width), BF), blk, pltpu.VMEM((2, 2, 8, width), F32)]
        + [
            dma((11, 4)), dma((11, 4)), dma((4,)), dma((4,)), dma((4,)), dma((2, 4)),
            dma((8, 4)), dma((8, 4)), dma((8, 5)), dma((8, 5)),
        ]
        + [pltpu.VMEM((8, 24, 128), F32), pltpu.VMEM((2, 16, 128), F32)]
        + [dma((4, 2)), dma((4, 2)), dma((4, 2)), dma((4,)), dma((8,)), dma((8,)), dma((2,)), dma((2,))],
        compiler_params=pltpu.CompilerParams(
            collective_id=0, has_side_effects=True, vmem_limit_bytes=56 * 2**20
        ),
        cost_estimate=pl.CostEstimate(flops=10**10, bytes_accessed=2**24, transcendentals=0),
    )(
        features, flat, norm_grads.reshape(16, 128), norm_m.reshape(2, 128), norm_v.reshape(2, 128), owners,
        moment1, moment2, left_stats, right_stats, left_basis, right_basis,
    )
    tile = pl.BlockSpec((1, slab, width), lambda i: (i, 0, 0))
    slots = pl.BlockSpec((1, 2, slab, width), lambda i: (i, 0, 0, 0))
    once2 = pl.BlockSpec((2, 128), lambda i: (0, 0))
    once16 = pl.BlockSpec((16, 128), lambda i: (0, 0))
    state = jax.ShapeDtypeStruct((nt, slab, width), F32)
    outs = pl.pallas_call(
        finish_kernel,
        grid=(nt,),
        out_shape=[state] * 6
        + [
            jax.ShapeDtypeStruct((4, 2, slab, width), BF),
            jax.ShapeDtypeStruct((2, 128), F32),
            jax.ShapeDtypeStruct((2, 128), F32),
            jax.ShapeDtypeStruct((16, 128), F32),
        ],
        in_specs=[tile] * 9 + [slots, once2, once2, once16],
        out_specs=[tile] * 6 + [slots, once2, once2, once16],
        cost_estimate=pl.CostEstimate(flops=2**20, bytes_accessed=2**23, transcendentals=0),
    )(moment1, moment2, left_stats, right_stats, rot, prod_l, prod_r, new_l, new_r, slot, nm, nv, ns)
    slot, nm, nv, ns = outs[6:]
    return (
        *outs[:6],
        slot.reshape(1, full, width),
        nm.reshape(norm_m.shape),
        nv.reshape(norm_v.shape),
        ns.reshape(1, -1),
    )


def solution(mesh):
    in_specs = (
        P("dp", None),
        P("dp", None, "mp"),
        P("dp", None),
        P(),
        P(None, "dp", "mp"),
        P(None, "dp", "mp"),
        P(None, "dp", "mp"),
        P(None, "dp", "mp"),
        P(None, "dp", "mp"),
        P(None, "dp", "mp"),
        P("dp"),
        P("dp"),
    )
    out_specs = (
        P(None, "dp", "mp"),
        P(None, "dp", "mp"),
        P(None, "dp", "mp"),
        P(None, "dp", "mp"),
        P(None, "dp", "mp"),
        P(None, "dp", "mp"),
        P("dp", None, "mp"),
        P("dp"),
        P("dp"),
        P("dp", None),
    )
    fused = mesh.shape["dp"] == 8 and mesh.shape["mp"] == 4
    body = fused_shards if fused else shards
    return jax.shard_map(body, mesh=mesh, in_specs=in_specs, out_specs=out_specs, check_vma=False)
```

```python
import jax
import jax.numpy as jnp
from jax import lax
from jax.experimental import pallas as pl
from jax.experimental.pallas import tpu as pltpu
from jax.sharding import PartitionSpec as P

MESH = pl.DeviceIdType.MESH

FIX_ONE = 1.0 - 0.9**10
FIX_TWO = 1.0 - 0.95**10
BF = jnp.bfloat16
F32 = jnp.float32


def dot(left, right, left_dim, right_dim):
    return lax.dot_general(
        left, right, (((left_dim,), (right_dim,)), ((), ())), preferred_element_type=F32
    )


contract = dot


def to_tile(blocks):
    out = lax.all_to_all(blocks, "mp", split_axis=1, concat_axis=1, tiled=True)
    k, n, r, c = out.shape
    return out.transpose(0, 2, 1, 3).reshape(k, r, n * c)


def to_home(rows, n):
    k, r, c = rows.shape
    out = rows.reshape(k, r, n, c // n).transpose(0, 2, 1, 3)
    return lax.all_to_all(out, "mp", split_axis=1, concat_axis=1, tiled=True)


def gather_rows(rows):
    return lax.all_gather(rows, "dp", axis=0, tiled=True)


def normalize(power):
    wide = power.astype(F32)
    return lax.rsqrt(jnp.sum(wide * wide, axis=0, keepdims=True) + 1e-06)


def shards(
    features,
    out_grads,
    norm_grads,
    owners,
    moment1,
    moment2,
    left_stats,
    right_stats,
    left_basis,
    right_basis,
    norm_m,
    norm_v,
):
    dp = lax.axis_size("dp")
    tiles, slab, width = moment1.shape
    full = slab * dp
    me = lax.axis_index("dp")
    row0 = me * slab

    narrow = to_tile(jnp.stack([left_basis, right_basis, left_stats, right_stats]).astype(BF))
    left_full = gather_rows(narrow[0])
    right_full = gather_rows(narrow[1])

    flat = out_grads.reshape(out_grads.shape[0], tiles * width)
    partial = contract(features, flat, 0, 0).astype(BF).reshape(dp, slab, tiles * width)
    parts = lax.all_to_all(partial, "dp", split_axis=0, concat_axis=0, tiled=True)
    grad_home = jnp.sum(parts.astype(F32), axis=0).astype(BF)
    grad_home = grad_home.reshape(slab, tiles, width).transpose(1, 0, 2)
    grad_rows = to_tile(grad_home[None])[0]
    grad_full = gather_rows(grad_rows)

    wide = to_tile(jnp.stack([moment1, moment2]))

    prod_l = contract(grad_rows, grad_full, 1, 1)
    grad_cols = lax.dynamic_slice_in_dim(grad_full, row0, slab, 1)
    prod_r = contract(grad_cols, grad_full, 0, 0)
    stats_l = (0.95 * narrow[2].astype(F32) + 0.05 * prod_l).astype(BF)
    stats_r = (0.95 * narrow[3].astype(F32) + 0.05 * prod_r).astype(BF)
    power_l = contract(stats_l, left_full, 1, 0).astype(BF)
    power_r = contract(stats_r, right_full, 1, 0).astype(BF)
    power_l_full = gather_rows(power_l)
    power_r_full = gather_rows(power_r)

    left_cols = lax.dynamic_slice_in_dim(left_full, row0, slab, 1)
    half = contract(left_cols, grad_full, 0, 0).astype(BF)
    rotated = contract(half, right_full, 1, 0)
    tile_one = 0.9 * wide[0] + 0.1 * rotated
    tile_two = 0.95 * wide[1] + 0.05 * rotated * rotated
    direction = (tile_one / FIX_ONE / (jnp.sqrt(tile_two / FIX_TWO) + 1e-08)).astype(BF)
    back = contract(direction, right_full, 1, 1).astype(BF)
    back_full = gather_rows(back)

    home1 = to_home(jnp.stack([rotated, prod_l, prod_r]).astype(BF), tiles).astype(F32)
    new_one = 0.9 * moment1 + 0.1 * home1[0]
    new_two = 0.95 * moment2 + 0.05 * home1[0] * home1[0]
    new_sl = 0.95 * left_stats + 0.05 * home1[1]
    new_sr = 0.95 * right_stats + 0.05 * home1[2]

    update = contract(narrow[0], back_full, 1, 0).astype(BF)

    def refine(power_full, power_rows):
        scale = normalize(power_full)
        iter_full = (power_full.astype(F32) * scale).astype(BF)
        iter_rows = (power_rows.astype(F32) * scale).astype(BF)
        gram = contract(iter_rows, iter_full, 1, 1).astype(BF)
        return 1.5 * iter_rows.astype(F32) - 0.5 * contract(gram, iter_full, 1, 0)

    new_l = refine(power_l_full, power_l)
    new_r = refine(power_r_full, power_r)
    home2 = to_home(jnp.stack([new_l.astype(BF), new_r.astype(BF), update]), tiles)
    new_bl = home2[0].astype(F32)
    new_br = home2[1].astype(F32)
    slot_of = jnp.arange(dp, dtype=jnp.int32)[:, None, None]
    slots = jnp.zeros((dp, slab, width), BF)
    for n in range(tiles):
        slots = jnp.where(slot_of == owners[n], home2[2, n][None], slots)
    update_slot = lax.all_to_all(slots, "dp", split_axis=0, concat_axis=0, tiled=True)
    update_slot = update_slot.reshape(1, full, width)

    norm_parts = norm_grads.reshape(dp, norm_m.shape[0])
    norm_parts = lax.all_to_all(norm_parts, "dp", split_axis=0, concat_axis=0, tiled=True)
    norm_total = jnp.sum(norm_parts, axis=0)
    new_nm = 0.9 * norm_m + 0.1 * norm_total
    new_nv = 0.95 * norm_v + 0.05 * norm_total * norm_total
    norm_step = new_nm / FIX_ONE / (jnp.sqrt(new_nv / FIX_TWO) + 1e-08)
    to_owner = (jnp.arange(dp, dtype=jnp.int32) == owners[tiles])[:, None]
    norm_out = jnp.where(to_owner, norm_step[None], 0.0)
    norm_slot = lax.all_to_all(norm_out, "dp", split_axis=0, concat_axis=0, tiled=True)
    norm_slot = norm_slot.reshape(1, -1)
    return (
        new_one,
        new_two,
        new_sl,
        new_sr,
        new_bl,
        new_br,
        update_slot,
        new_nm,
        new_nv,
        norm_slot,
    )


def fused_kernel(
    feat_hbm, og_hbm, ng_ref, nmi_ref, nvi_ref, own_ref, m1_hbm, m2_hbm, sl_hbm, sr_hbm, lb_hbm, rb_hbm,
    rot_home, pl_home, pr_home, nl_home, nr_home, upd_out, nm_out, nv_out, ns_out,
    feat_ref, og_ref, m1_ref, m2_ref, sl_ref, sr_ref, lb_ref, rb_ref, pack_ref, in_sem,
    ft, ppart, own, xrecv, line, lsend,
    zl, zr, zsl, zsr, zm1, zm2,
    L, R, G, DIR, IL, IR, SL, SR, PL, PR, m1t, m2t, rot_s, nl_s, nr_s, upd, upd_px, sq,
    zs_send, zs_recv, x_send, x_recv, ln_send, ln_recv, ga_send, ga_recv, co_send, co_recv,
    norm_all, nscr, up_r, up_l, up_recv, ux_sem, nm_send, nm_recv, sq_send, sq_recv,
):
    nt, slab, width = m1_ref.shape
    dp = lax.axis_index("dp")
    q = lax.axis_index("mp")
    z, x = dp // 2, lax.rem(dp, 2)
    y, c = q // 2, lax.rem(q, 2)
    half = 4 * slab

    def at(zz, xx, yy, cc):
        return (zz * 2 + xx, yy * 2 + cc)

    def cols(yy, cc):
        return pl.ds(pl.multiple_of((yy * 2 + cc) * width, width), width)

    mycols = cols(y, c)

    def remote(src, dst, ssem, rsem, dev):
        return pltpu.make_async_remote_copy(
            src_ref=src, dst_ref=dst, send_sem=ssem, recv_sem=rsem, device_id=dev, device_id_type=MESH
        )

    pending = []

    def start(cp):
        cp.start()
        pending.append(cp)

    def zspread(kind, src, dst):
        for j in (1, 2, 3):
            zz = lax.rem(z + j, 4)
            start(remote(src(zz), dst(z), zs_send.at[kind, j], zs_recv.at[kind, z], at(zz, x, y, c)))

    def zwait(kind, src, dst):
        for j in (1, 2, 3):
            zz = lax.rem(z + j, 4)
            remote(src(zz), dst(zz), zs_send.at[kind, j], zs_recv.at[kind, zz], at(zz, x, y, c)).wait_recv()

    xdev, ydev, cdev = at(z, 1 - x, y, c), at(z, x, 1 - y, c), at(z, x, y, 1 - c)

    def ga(kind, slot, ref, dev):
        return remote(ref, ref, ga_send.at[kind, slot], ga_recv.at[kind, slot], dev)

    def co(kind, slot, ref):
        return remote(ref, ref, co_send.at[kind, slot], co_recv.at[kind, slot], cdev)

    def gstart(kind, blk):
        b = blk(x, y, c, 0, 4)
        start(ga(kind, 0, b, xdev))
        start(ga(kind, 1, b, ydev))
        start(co(kind, 0, b))

    def gmid(kind, blk):
        ga(kind, 0, blk(1 - x, y, c, 0, 4), xdev).wait_recv()
        start(ga(kind, 2, blk(1 - x, y, c, 0, 2), ydev))
        start(co(kind, 1, blk(1 - x, y, c, 0, 4)))
        ga(kind, 1, blk(x, 1 - y, c, 0, 4), ydev).wait_recv()
        start(ga(kind, 3, blk(x, 1 - y, c, 2, 4), xdev))
        start(co(kind, 2, blk(x, 1 - y, c, 0, 4)))

    def gend(kind, blk):
        ga(kind, 2, blk(1 - x, 1 - y, c, 0, 2), ydev).wait_recv()
        start(co(kind, 3, blk(1 - x, 1 - y, c, 0, 2)))
        ga(kind, 3, blk(1 - x, 1 - y, c, 2, 4), xdev).wait_recv()
        start(co(kind, 4, blk(1 - x, 1 - y, c, 2, 4)))
        co(kind, 0, blk(x, y, 1 - c, 0, 4)).wait_recv()
        co(kind, 1, blk(1 - x, y, 1 - c, 0, 4)).wait_recv()
        co(kind, 2, blk(x, 1 - y, 1 - c, 0, 4)).wait_recv()
        co(kind, 3, blk(1 - x, 1 - y, 1 - c, 0, 2)).wait_recv()
        co(kind, 4, blk(1 - x, 1 - y, 1 - c, 2, 4)).wait_recv()

    def inter(ref):
        return lambda xx, yy, cc, a, b: ref.at[pl.ds(a, b - a), xx, :, cols(yy, cc)]

    def halves(ref):
        def blk(xx, yy, cc, a, b):
            if b - a == 4:
                return ref.at[pl.ds(2 * xx, 2), :, :, cols(yy, cc)]
            return ref.at[2 * xx + a // 2, :, :, cols(yy, cc)]

        return blk

    def bstart(kind, ref, part):
        start(ga(kind, 0, ref.at[:, x, :, mycols], xdev))
        start(ga(kind, 1, part(ref, 1 - y, x, y, c), ydev))
        start(co(kind, 0, part(ref, y, x, y, c)))

    def bx(kind, ref, part):
        ga(kind, 0, ref.at[:, 1 - x, :, mycols], xdev).wait_recv()
        start(ga(kind, 2, part(ref, 1 - y, 1 - x, y, c), ydev))
        start(co(kind, 1, part(ref, y, 1 - x, y, c)))

    def bc(kind, ref, part):
        ga(kind, 1, part(ref, y, x, 1 - y, c), ydev).wait_recv()
        start(co(kind, 2, part(ref, y, x, 1 - y, c)))
        ga(kind, 2, part(ref, y, 1 - x, 1 - y, c), ydev).wait_recv()
        start(co(kind, 3, part(ref, y, 1 - x, 1 - y, c)))

    def bend(kind, ref, part):
        for n, (xx, yy) in enumerate(((x, y), (1 - x, y), (x, 1 - y), (1 - x, 1 - y))):
            co(kind, n, part(ref, y, xx, yy, 1 - c)).wait_recv()

    def allrows(ref, to_y, xx, yy, cc):
        return ref.at[:, xx, :, cols(yy, cc)]

    def tworows(ref, to_y, xx, yy, cc):
        return ref.at[pl.ds(2 * to_y, 2), xx, :, cols(yy, cc)]

    def rstart(kind, rowref):
        b = rowref(y, c)
        start(ga(kind, 0, b, ydev))
        start(co(kind, 0, b))

    def rmid(kind, rowref):
        ga(kind, 0, rowref(1 - y, c), ydev).wait_recv()
        start(co(kind, 1, rowref(1 - y, c)))

    def rend(kind, rowref):
        co(kind, 0, rowref(y, 1 - c)).wait_recv()
        co(kind, 1, rowref(1 - y, 1 - c)).wait_recv()

    def srows(ref):
        return lambda yy, cc: ref.at[:, :, cols(yy, cc)]

    def xrows(ref):
        return lambda yy, cc: ref.at[:, x, :, cols(yy, cc)]

    barrier = pltpu.get_barrier_semaphore()
    peers = [(lax.rem(dp + j, 8), q) for j in range(1, 8)]
    peers += [at(z, x, 1 - y, c), at(z, 1 - x, 1 - y, c), at(z, x, y, 1 - c)]
    for peer in peers:
        pl.semaphore_signal(barrier, inc=1, device_id=peer, device_id_type=MESH)

    loads = {}
    for n, (src, dst) in enumerate((
        (feat_hbm, feat_ref), (og_hbm, og_ref), (lb_hbm, lb_ref), (rb_hbm, rb_ref),
        (m1_hbm, m1_ref), (m2_hbm, m2_ref), (sl_hbm, sl_ref), (sr_hbm, sr_ref),
    )):
        loads[n] = pltpu.make_async_copy(src, dst, in_sem.at[n])
        loads[n].start()
    pack_ref[0:16] = ng_ref[...]
    pack_ref[16:18] = nmi_ref[...]
    pack_ref[18:20] = nvi_ref[...]
    pack_ref[20:24] = jnp.zeros((4, 128), F32)
    norm_all[dp] = pack_ref[...]
    loads[0].wait()
    ft[...] = feat_ref[:, pl.ds(pl.multiple_of((1 - x) * half, half), half)].T
    loads[1].wait()

    def tile_of(k):
        zz = jnp.minimum(z, 3 - z)
        base = (3, 2, 1 - zz, zz)[k]
        return jnp.where(z < 2, base, 3 - base)

    def og(t):
        return og_ref[:, pl.ds(pl.multiple_of(t * width, width), width)]

    def partial(k):
        t = tile_of(k)
        ppart[t] = dot(ft[...], og(t), 1, 0).astype(BF)

    def xsend(k):
        t = tile_of(k)
        start(remote(ppart.at[t], xrecv.at[t], x_send.at[t], x_recv.at[t], xdev))

    partial(0)
    loads[2].wait()
    loads[3].wait()
    zl[...] = lb_ref[...].astype(BF)
    zr[...] = rb_ref[...].astype(BF)
    L[z, x, :, mycols] = zl[z]
    R[z, x, :, mycols] = zr[z]
    pl.semaphore_wait(barrier, len(peers))

    def tile_in(src, dst):
        return (lambda zz: src.at[zz]), dst

    lz = tile_in(zl, lambda s: L.at[s, x, :, mycols])
    rz = tile_in(zr, lambda s: R.at[s, x, :, mycols])
    xsend(0)
    zspread(0, *lz)
    zspread(1, *rz)
    partial(1)
    xsend(1)
    partial(2)
    partial(3)
    for j in range(1, 8):
        dd = lax.rem(dp + j, 8)
        start(remote(pack_ref, norm_all.at[dp], nm_send.at[j], nm_recv.at[dp], (dd, q)))
    ft[...] = feat_ref[:, pl.ds(pl.multiple_of(x * half, half), half)].T
    for k in range(4):
        t = tile_of(k)
        own[t] = dot(ft[...], og(t), 1, 0)
    for n in range(4, 8):
        loads[n].wait()
    zsl[...] = sl_ref[...].astype(BF)
    zsr[...] = sr_ref[...].astype(BF)
    zm1[...] = m1_ref[...].astype(BF)
    zm2[...] = m2_ref[...].astype(BF)
    SL[z, :, mycols] = zsl[z]
    SR[z, :, mycols] = zsr[z]
    m1t[z] = zm1[z]
    m2t[z] = zm2[z]

    def xwait(t):
        remote(ppart.at[t], xrecv.at[t], x_send.at[t], x_recv.at[t], at(z, 1 - x, y, c)).wait_recv()

    def lwait(d, t):
        remote(lsend.at[t], line.at[d, t], ln_send.at[t], ln_recv.at[d, t], at(z, x, y, 1 - c)).wait_recv()

    slz = tile_in(zsl, lambda s: SL.at[s, :, mycols])
    srz = tile_in(zsr, lambda s: SR.at[s, :, mycols])
    m1z = tile_in(zm1, lambda s: m1t.at[s])
    m2z = tile_in(zm2, lambda s: m2t.at[s])

    def hop(k):
        t = tile_of(k)
        right = t > z
        d = jnp.where(right, 0, 1)
        zn = jnp.where(right, z + 1, z - 1)
        inner_hop = jnp.where(right, z > 0, z < 3)
        xwait(t)
        own[t] += xrecv[t].astype(F32)

        @pl.when(inner_hop)
        def _():
            lwait(d, t)
            lsend[t] = (own[t] + line[d, t].astype(F32)).astype(BF)

        @pl.when(jnp.logical_not(inner_hop))
        def _():
            lsend[t] = own[t].astype(BF)

        start(remote(lsend.at[t], line.at[d, t], ln_send.at[t], ln_recv.at[d, t], at(zn, x, y, c)))

    zwait(0, *lz)
    bstart(0, L, allrows)
    xsend(2)
    hop(0)
    zwait(1, *rz)
    bstart(1, R, tworows)
    xsend(3)
    hop(1)
    bx(0, L, allrows)
    hop(2)
    zspread(2, *slz)
    zspread(3, *srz)
    zspread(4, *m1z)
    zspread(5, *m2z)
    bx(1, R, tworows)
    bc(0, L, allrows)
    xwait(z)
    own[z] += xrecv[z].astype(F32)

    @pl.when(z > 0)
    def _():
        lwait(0, z)
        own[z] += line[0, z].astype(F32)

    @pl.when(z < 3)
    def _():
        lwait(1, z)
        own[z] += line[1, z].astype(F32)

    G[pl.ds(2 * x, 2), :, :, mycols] = own[z].astype(BF).reshape(2, 2, slab, width)
    gstart(2, halves(G))
    gmid(2, halves(G))
    zwait(2, *slz)
    rstart(6, srows(SL))
    zwait(3, *srz)
    rstart(7, srows(SR))
    bc(1, R, tworows)
    bend(0, L, allrows)
    bend(1, R, tworows)
    gend(2, halves(G))
    zwait(4, *m1z)
    zwait(5, *m2z)

    def full(ref):
        return ref[...].reshape(8 * slab, 8 * slab)

    def rows(ref):
        return ref[:, x].reshape(half, 8 * slab)

    def colb(ref):
        return ref[:, :, :, mycols].reshape(8 * slab, width)

    def lane(ref, zz):
        return ref[:, :, :, pl.ds(pl.multiple_of((2 * zz + x) * slab, slab), slab)].reshape(8 * slab, slab)

    inner = dot(full(G), colb(R), 1, 0).astype(BF)
    for s in range(4):
        rotated = dot(lane(L, s), inner, 0, 0)
        rot_s[s] = rotated.astype(BF)
        one = 0.9 * m1t[s].astype(F32) + 0.1 * rotated
        two = 0.95 * m2t[s].astype(F32) + 0.05 * rotated * rotated
        DIR[s, x, :, mycols] = (one / FIX_ONE / (jnp.sqrt(two / FIX_TWO) + 1e-08)).astype(BF)
    gstart(3, inter(DIR))
    rot_home[z] = rot_s[z]
    rotz = tile_in(rot_s, lambda s: rot_home.at[s])
    zspread(6, *rotz)

    def power(prods, stat, basis, prod, slot):
        prods[...] = prod.astype(BF)
        stats = (0.95 * stat[...].astype(F32) + 0.05 * prods[...].astype(F32)).astype(BF)
        out = dot(stats.reshape(half, 8 * slab), colb(basis), 1, 0)
        total = jnp.sum(out * out, axis=0, keepdims=True)
        sq[0, slot] = jnp.broadcast_to(total, (8, width))
        start(remote(sq.at[0, slot], sq.at[1, slot], sq_send.at[slot], sq_recv.at[slot], at(z, 1 - x, y, c)))
        return out

    def iterate(out, slot, it):
        remote(sq.at[0, slot], sq.at[1, slot], sq_send.at[slot], sq_recv.at[slot], at(z, 1 - x, y, c)).wait_recv()
        total = (sq[0, slot] + sq[1, slot])[0:1]
        it[:, x, :, mycols] = (out * lax.rsqrt(total + 1e-06)).astype(BF).reshape(4, slab, width)

    rmid(6, srows(SL))
    prod_l = dot(rows(G), full(G), 1, 1).reshape(4, slab, 8 * slab)
    rend(6, srows(SL))
    pow_l = power(PL, SL, L, prod_l, 0)
    pl_home[z] = PL[z, :, mycols]
    plz = (lambda zz: PL.at[zz, :, mycols]), (lambda s: pl_home.at[s])
    zspread(7, *plz)
    rmid(7, srows(SR))
    for s in range(4):
        PR[s] = dot(lane(G, s), full(G), 0, 0).astype(BF)
    rend(7, srows(SR))
    pow_r = power(PR, SR, R, PR[...], 1)
    pr_home[z] = PR[z, :, mycols]
    prz = (lambda zz: PR.at[zz, :, mycols]), (lambda s: pr_home.at[s])
    zspread(8, *prz)
    iterate(pow_l, 0, IL)
    gmid(3, inter(DIR))
    gstart(4, inter(IL))
    iterate(pow_r, 1, IR)
    gstart(5, inter(IR))

    gend(3, inter(DIR))
    back = dot(full(DIR), R[q].reshape(2 * slab, 8 * slab), 1, 1).astype(BF)
    upd[z] = dot(rows(L), back, 1, 0).astype(BF).reshape(4, slab, width)

    def ucopy(t, h, right):
        zn = jnp.clip(z + 1 if right else z - 1, 0, 3)
        part = upd.at[t, pl.ds(2 * h, 2)]
        return remote(part, part, (up_r if right else up_l).at[t, h], up_recv.at[t, h], at(zn, x, y, c))

    def upd_on(t, h, right):
        @pl.when(z < 3 if right else z > 0)
        def _():
            ucopy(t, h, right).start()

    for h in range(2):
        upd_on(z, h, True)
        upd_on(z, h, False)
    gmid(4, inter(IL))

    def refine(it, kind, out_s, home, zk):
        gend(kind, inter(it))
        gram = dot(rows(it), full(it), 1, 1).astype(BF)
        mine = it[:, x, :, mycols].reshape(half, width).astype(F32)
        new = 1.5 * mine - 0.5 * dot(gram, colb(it), 1, 0)
        out_s[...] = new.astype(BF).reshape(4, slab, width)
        home[z] = out_s[z]
        mv = tile_in(out_s, lambda s: home.at[s])
        return mv

    def relay(j, h):
        @pl.when(z - j >= 0)
        def _():
            t = jnp.maximum(z - j, 0)
            ucopy(t, h, True).wait_recv()
            upd_on(t, h, True)

        @pl.when(z + j <= 3)
        def _():
            t = jnp.minimum(z + j, 3)
            ucopy(t, h, False).wait_recv()
            upd_on(t, h, False)

    gmid(5, inter(IR))
    relay(1, 0)
    relay(1, 1)
    nlz = refine(IL, 4, nl_s, nl_home, 9)
    relay(2, 0)
    relay(2, 1)
    nrz = refine(IR, 5, nr_s, nr_home, 10)
    relay(3, 0)
    relay(3, 1)
    zspread(9, *nlz)
    zspread(10, *nrz)

    def pick(who, h):
        got = jnp.zeros((2, slab, width), BF)
        for t in range(4):
            got = jnp.where(own_ref[t] == who, upd[t, 2 * h : 2 * h + 2], got)
        return got

    def ucross(h, to):
        return remote(
            upd_px.at[2 * h : 2 * h + 2], upd_out.at[2 * h : 2 * h + 2, to], ux_sem.at[h], ux_sem.at[2 + h], xdev
        )

    for h in range(2):
        upd_px[2 * h : 2 * h + 2] = pick(z * 2 + 1 - x, h)
        start(ucross(h, x))
        upd_out[2 * h : 2 * h + 2, x] = pick(dp, h)
    for j in range(1, 8):
        dd = lax.rem(dp + j, 8)
        remote(pack_ref, norm_all.at[dd], nm_send.at[j], nm_recv.at[dd], (dd, q)).wait_recv()
    for j in range(8):
        nscr[0, 2 * j : 2 * j + 2] = norm_all[j, 16:18]
        nscr[1, 2 * j : 2 * j + 2] = norm_all[j, 18:20]
    total = jnp.sum(norm_all[:, 0:16], axis=0)
    nm = 0.9 * nscr[0] + 0.1 * total
    nv = 0.95 * nscr[1] + 0.05 * total * total
    step = nm / FIX_ONE / (jnp.sqrt(nv / FIX_TWO) + 1e-08)
    ns_out[...] = jnp.where(own_ref[nt] == dp, step, jnp.zeros_like(step))
    nscr[0] = nm
    nscr[1] = nv
    nm_out[...] = nscr[0, pl.ds(2 * dp, 2)]
    nv_out[...] = nscr[1, pl.ds(2 * dp, 2)]
    zwait(6, *rotz)
    zwait(7, *plz)
    zwait(8, *prz)
    zwait(9, *nlz)
    zwait(10, *nrz)
    for h in range(2):
        ucross(h, 1 - x).wait_recv()

    @pl.when(z < 3)
    def _():
        for j in range(4):
            @pl.when(z - j >= 0)
            def _():
                for h in range(2):
                    ucopy(jnp.maximum(z - j, 0), h, True).wait_send()

    @pl.when(z > 0)
    def _():
        for j in range(4):
            @pl.when(z + j <= 3)
            def _():
                for h in range(2):
                    ucopy(jnp.minimum(z + j, 3), h, False).wait_send()

    for cp in pending:
        cp.wait_send()


def finish_kernel(
    m1, m2, sl, sr, rot, prod_l, prod_r, new_l, new_r, slot, nm, nv, ns,
    m1_out, m2_out, sl_out, sr_out, bl_out, br_out, slot_out, nm_out, nv_out, ns_out,
):
    turned = rot[...].astype(F32)
    m1_out[...] = 0.9 * m1[...] + 0.1 * turned
    m2_out[...] = 0.95 * m2[...] + 0.05 * turned * turned
    sl_out[...] = 0.95 * sl[...] + 0.05 * prod_l[...].astype(F32)
    sr_out[...] = 0.95 * sr[...] + 0.05 * prod_r[...].astype(F32)
    bl_out[...] = new_l[...].astype(F32)
    br_out[...] = new_r[...].astype(F32)
    slot_out[...] = slot[...]
    nm_out[...] = nm[...]
    nv_out[...] = nv[...]
    ns_out[...] = ns[...]


def fused_shards(
    features,
    out_grads,
    norm_grads,
    owners,
    moment1,
    moment2,
    left_stats,
    right_stats,
    left_basis,
    right_basis,
    norm_m,
    norm_v,
):
    nt, slab, width = moment1.shape
    full = 8 * slab
    flat = out_grads.reshape(out_grads.shape[0], nt * width)
    vm = pl.BlockSpec(memory_space=pltpu.VMEM)
    hbm = pl.BlockSpec(memory_space=pl.ANY)
    home = jax.ShapeDtypeStruct((nt, slab, width), BF)
    big = pltpu.VMEM((4, 2, slab, full), BF)
    blk = pltpu.VMEM((4, slab, width), BF)
    piece = (4 * slab, width)
    dma = pltpu.SemaphoreType.DMA
    rot, prod_l, prod_r, new_l, new_r, slot, nm, nv, ns = pl.pallas_call(
        fused_kernel,
        out_shape=[home] * 5
        + [
            jax.ShapeDtypeStruct((4, 2, slab, width), BF),
            jax.ShapeDtypeStruct((2, 128), F32),
            jax.ShapeDtypeStruct((2, 128), F32),
            jax.ShapeDtypeStruct((16, 128), F32),
        ],
        in_specs=[hbm] * 2 + [vm] * 3 + [pl.BlockSpec(memory_space=pltpu.SMEM)] + [hbm] * 6,
        out_specs=[vm] * 9,
        scratch_shapes=[
            pltpu.VMEM(features.shape, BF),
            pltpu.VMEM(flat.shape, BF),
        ]
        + [pltpu.VMEM((nt, slab, width), F32)] * 6
        + [pltpu.VMEM((24, 128), F32), dma((8,))]
        + [
            pltpu.VMEM((4 * slab, features.shape[0]), BF),
            pltpu.VMEM((4,) + piece, BF),
            pltpu.VMEM((4,) + piece, F32),
            pltpu.VMEM((4,) + piece, BF),
            pltpu.VMEM((2, 4) + piece, BF),
            pltpu.VMEM((4,) + piece, BF),
        ]
        + [blk] * 6
        + [big] * 6
        + [pltpu.VMEM((4, slab, full), BF)] * 4
        + [blk] * 5
        + [pltpu.VMEM((4, 4, slab, width), BF), blk, pltpu.VMEM((2, 2, 8, width), F32)]
        + [
            dma((11, 4)), dma((11, 4)), dma((4,)), dma((4,)), dma((4,)), dma((2, 4)),
            dma((8, 4)), dma((8, 4)), dma((8, 5)), dma((8, 5)),
        ]
        + [pltpu.VMEM((8, 24, 128), F32), pltpu.VMEM((2, 16, 128), F32)]
        + [dma((4, 2)), dma((4, 2)), dma((4, 2)), dma((4,)), dma((8,)), dma((8,)), dma((2,)), dma((2,))],
        compiler_params=pltpu.CompilerParams(
            collective_id=0, has_side_effects=True, vmem_limit_bytes=56 * 2**20
        ),
        cost_estimate=pl.CostEstimate(flops=10**10, bytes_accessed=2**24, transcendentals=0),
    )(
        features, flat, norm_grads.reshape(16, 128), norm_m.reshape(2, 128), norm_v.reshape(2, 128), owners,
        moment1, moment2, left_stats, right_stats, left_basis, right_basis,
    )
    tile = pl.BlockSpec((1, slab, width), lambda i: (i, 0, 0))
    slots = pl.BlockSpec((1, 2, slab, width), lambda i: (i, 0, 0, 0))
    once2 = pl.BlockSpec((2, 128), lambda i: (0, 0))
    once16 = pl.BlockSpec((16, 128), lambda i: (0, 0))
    state = jax.ShapeDtypeStruct((nt, slab, width), F32)
    outs = pl.pallas_call(
        finish_kernel,
        grid=(nt,),
        out_shape=[state] * 6
        + [
            jax.ShapeDtypeStruct((4, 2, slab, width), BF),
            jax.ShapeDtypeStruct((2, 128), F32),
            jax.ShapeDtypeStruct((2, 128), F32),
            jax.ShapeDtypeStruct((16, 128), F32),
        ],
        in_specs=[tile] * 9 + [slots, once2, once2, once16],
        out_specs=[tile] * 6 + [slots, once2, once2, once16],
        cost_estimate=pl.CostEstimate(flops=2**20, bytes_accessed=2**23, transcendentals=0),
    )(moment1, moment2, left_stats, right_stats, rot, prod_l, prod_r, new_l, new_r, slot, nm, nv, ns)
    slot, nm, nv, ns = outs[6:]
    return (
        *outs[:6],
        slot.reshape(1, full, width),
        nm.reshape(norm_m.shape),
        nv.reshape(norm_v.shape),
        ns.reshape(1, -1),
    )


def solution(mesh):
    in_specs = (
        P("dp", None),
        P("dp", None, "mp"),
        P("dp", None),
        P(),
        P(None, "dp", "mp"),
        P(None, "dp", "mp"),
        P(None, "dp", "mp"),
        P(None, "dp", "mp"),
        P(None, "dp", "mp"),
        P(None, "dp", "mp"),
        P("dp"),
        P("dp"),
    )
    out_specs = (
        P(None, "dp", "mp"),
        P(None, "dp", "mp"),
        P(None, "dp", "mp"),
        P(None, "dp", "mp"),
        P(None, "dp", "mp"),
        P(None, "dp", "mp"),
        P("dp", None, "mp"),
        P("dp"),
        P("dp"),
        P("dp", None),
    )
    fused = mesh.shape["dp"] == 8 and mesh.shape["mp"] == 4
    body = fused_shards if fused else shards
    return jax.shard_map(body, mesh=mesh, in_specs=in_specs, out_specs=out_specs, check_vma=False)
```

```python
import jax
import jax.numpy as jnp
from jax import lax
from jax.experimental import pallas as pl
from jax.experimental.pallas import tpu as pltpu
from jax.sharding import PartitionSpec as P

MESH = pl.DeviceIdType.MESH

FIX_ONE = 1.0 - 0.9**10
FIX_TWO = 1.0 - 0.95**10
BF = jnp.bfloat16
F32 = jnp.float32


def dot(left, right, left_dim, right_dim):
    return lax.dot_general(
        left, right, (((left_dim,), (right_dim,)), ((), ())), preferred_element_type=F32
    )


contract = dot


def to_tile(blocks):
    out = lax.all_to_all(blocks, "mp", split_axis=1, concat_axis=1, tiled=True)
    k, n, r, c = out.shape
    return out.transpose(0, 2, 1, 3).reshape(k, r, n * c)


def to_home(rows, n):
    k, r, c = rows.shape
    out = rows.reshape(k, r, n, c // n).transpose(0, 2, 1, 3)
    return lax.all_to_all(out, "mp", split_axis=1, concat_axis=1, tiled=True)


def gather_rows(rows):
    return lax.all_gather(rows, "dp", axis=0, tiled=True)


def normalize(power):
    wide = power.astype(F32)
    return lax.rsqrt(jnp.sum(wide * wide, axis=0, keepdims=True) + 1e-06)


def shards(
    features,
    out_grads,
    norm_grads,
    owners,
    moment1,
    moment2,
    left_stats,
    right_stats,
    left_basis,
    right_basis,
    norm_m,
    norm_v,
):
    dp = lax.axis_size("dp")
    tiles, slab, width = moment1.shape
    full = slab * dp
    me = lax.axis_index("dp")
    row0 = me * slab

    narrow = to_tile(jnp.stack([left_basis, right_basis, left_stats, right_stats]).astype(BF))
    left_full = gather_rows(narrow[0])
    right_full = gather_rows(narrow[1])

    flat = out_grads.reshape(out_grads.shape[0], tiles * width)
    partial = contract(features, flat, 0, 0).astype(BF).reshape(dp, slab, tiles * width)
    parts = lax.all_to_all(partial, "dp", split_axis=0, concat_axis=0, tiled=True)
    grad_home = jnp.sum(parts.astype(F32), axis=0).astype(BF)
    grad_home = grad_home.reshape(slab, tiles, width).transpose(1, 0, 2)
    grad_rows = to_tile(grad_home[None])[0]
    grad_full = gather_rows(grad_rows)

    wide = to_tile(jnp.stack([moment1, moment2]))

    prod_l = contract(grad_rows, grad_full, 1, 1)
    grad_cols = lax.dynamic_slice_in_dim(grad_full, row0, slab, 1)
    prod_r = contract(grad_cols, grad_full, 0, 0)
    stats_l = (0.95 * narrow[2].astype(F32) + 0.05 * prod_l).astype(BF)
    stats_r = (0.95 * narrow[3].astype(F32) + 0.05 * prod_r).astype(BF)
    power_l = contract(stats_l, left_full, 1, 0).astype(BF)
    power_r = contract(stats_r, right_full, 1, 0).astype(BF)
    power_l_full = gather_rows(power_l)
    power_r_full = gather_rows(power_r)

    left_cols = lax.dynamic_slice_in_dim(left_full, row0, slab, 1)
    half = contract(left_cols, grad_full, 0, 0).astype(BF)
    rotated = contract(half, right_full, 1, 0)
    tile_one = 0.9 * wide[0] + 0.1 * rotated
    tile_two = 0.95 * wide[1] + 0.05 * rotated * rotated
    direction = (tile_one / FIX_ONE / (jnp.sqrt(tile_two / FIX_TWO) + 1e-08)).astype(BF)
    back = contract(direction, right_full, 1, 1).astype(BF)
    back_full = gather_rows(back)

    home1 = to_home(jnp.stack([rotated, prod_l, prod_r]).astype(BF), tiles).astype(F32)
    new_one = 0.9 * moment1 + 0.1 * home1[0]
    new_two = 0.95 * moment2 + 0.05 * home1[0] * home1[0]
    new_sl = 0.95 * left_stats + 0.05 * home1[1]
    new_sr = 0.95 * right_stats + 0.05 * home1[2]

    update = contract(narrow[0], back_full, 1, 0).astype(BF)

    def refine(power_full, power_rows):
        scale = normalize(power_full)
        iter_full = (power_full.astype(F32) * scale).astype(BF)
        iter_rows = (power_rows.astype(F32) * scale).astype(BF)
        gram = contract(iter_rows, iter_full, 1, 1).astype(BF)
        return 1.5 * iter_rows.astype(F32) - 0.5 * contract(gram, iter_full, 1, 0)

    new_l = refine(power_l_full, power_l)
    new_r = refine(power_r_full, power_r)
    home2 = to_home(jnp.stack([new_l.astype(BF), new_r.astype(BF), update]), tiles)
    new_bl = home2[0].astype(F32)
    new_br = home2[1].astype(F32)
    slot_of = jnp.arange(dp, dtype=jnp.int32)[:, None, None]
    slots = jnp.zeros((dp, slab, width), BF)
    for n in range(tiles):
        slots = jnp.where(slot_of == owners[n], home2[2, n][None], slots)
    update_slot = lax.all_to_all(slots, "dp", split_axis=0, concat_axis=0, tiled=True)
    update_slot = update_slot.reshape(1, full, width)

    norm_parts = norm_grads.reshape(dp, norm_m.shape[0])
    norm_parts = lax.all_to_all(norm_parts, "dp", split_axis=0, concat_axis=0, tiled=True)
    norm_total = jnp.sum(norm_parts, axis=0)
    new_nm = 0.9 * norm_m + 0.1 * norm_total
    new_nv = 0.95 * norm_v + 0.05 * norm_total * norm_total
    norm_step = new_nm / FIX_ONE / (jnp.sqrt(new_nv / FIX_TWO) + 1e-08)
    to_owner = (jnp.arange(dp, dtype=jnp.int32) == owners[tiles])[:, None]
    norm_out = jnp.where(to_owner, norm_step[None], 0.0)
    norm_slot = lax.all_to_all(norm_out, "dp", split_axis=0, concat_axis=0, tiled=True)
    norm_slot = norm_slot.reshape(1, -1)
    return (
        new_one,
        new_two,
        new_sl,
        new_sr,
        new_bl,
        new_br,
        update_slot,
        new_nm,
        new_nv,
        norm_slot,
    )


def fused_kernel(
    feat_hbm, og_hbm, ng_ref, nmi_ref, nvi_ref, own_ref, m1_hbm, m2_hbm, sl_hbm, sr_hbm, lb_hbm, rb_hbm,
    rot_home, pl_home, pr_home, nl_home, nr_home, upd_out, nm_out, nv_out, ns_out,
    feat_ref, og_ref, m1_ref, m2_ref, sl_ref, sr_ref, lb_ref, rb_ref, pack_ref, in_sem,
    ft, ppart, own, xrecv, line, lsend,
    zl, zr, zsl, zsr, zm1, zm2,
    L, R, G, DIR, IL, IR, SL, SR, PL, PR, m1t, m2t, rot_s, nl_s, nr_s, upd, upd_px, sq,
    zs_send, zs_recv, x_send, x_recv, ln_send, ln_recv, ga_send, ga_recv, co_send, co_recv,
    norm_all, nscr, up_r, up_l, up_recv, ux_sem, nm_send, nm_recv, sq_send, sq_recv,
):
    nt, slab, width = m1_ref.shape
    dp = lax.axis_index("dp")
    q = lax.axis_index("mp")
    z, x = dp // 2, lax.rem(dp, 2)
    y, c = q // 2, lax.rem(q, 2)
    half = 4 * slab

    def at(zz, xx, yy, cc):
        return (zz * 2 + xx, yy * 2 + cc)

    def cols(yy, cc):
        return pl.ds(pl.multiple_of((yy * 2 + cc) * width, width), width)

    mycols = cols(y, c)

    def remote(src, dst, ssem, rsem, dev):
        return pltpu.make_async_remote_copy(
            src_ref=src, dst_ref=dst, send_sem=ssem, recv_sem=rsem, device_id=dev, device_id_type=MESH
        )

    pending = []

    def start(cp):
        cp.start()
        pending.append(cp)

    def zspread(kind, src, dst):
        for j in (1, 2, 3):
            zz = lax.rem(z + j, 4)
            start(remote(src(zz), dst(z), zs_send.at[kind, j], zs_recv.at[kind, z], at(zz, x, y, c)))

    def zwait(kind, src, dst):
        for j in (1, 2, 3):
            zz = lax.rem(z + j, 4)
            remote(src(zz), dst(zz), zs_send.at[kind, j], zs_recv.at[kind, zz], at(zz, x, y, c)).wait_recv()

    def zspread_if(cond, kind, src, dst):
        @pl.when(cond)
        def _():
            for j in (1, 2, 3):
                zz = lax.rem(z + j, 4)
                remote(src(zz), dst(z), zs_send.at[kind, j], zs_recv.at[kind, z], at(zz, x, y, c)).start()

    def zsent(kind, src, dst):
        for j in (1, 2, 3):
            zz = lax.rem(z + j, 4)
            remote(src(zz), dst(z), zs_send.at[kind, j], zs_recv.at[kind, z], at(zz, x, y, c)).wait_send()

    xdev, ydev, cdev = at(z, 1 - x, y, c), at(z, x, 1 - y, c), at(z, x, y, 1 - c)

    def ga(kind, slot, ref, dev):
        return remote(ref, ref, ga_send.at[kind, slot], ga_recv.at[kind, slot], dev)

    def co(kind, slot, ref):
        return remote(ref, ref, co_send.at[kind, slot], co_recv.at[kind, slot], cdev)

    def gstart(kind, blk):
        start(ga(kind, 0, blk(x, y, c, 0, 2), xdev))
        start(ga(kind, 1, blk(x, y, c, 2, 4), ydev))
        start(ga(kind, 4, blk(x, y, c, 2, 4), xdev))
        start(ga(kind, 5, blk(x, y, c, 0, 2), ydev))
        start(co(kind, 0, blk(x, y, c, 0, 4)))

    def gmid(kind, blk):
        ga(kind, 0, blk(1 - x, y, c, 0, 2), xdev).wait_recv()
        start(ga(kind, 2, blk(1 - x, y, c, 0, 2), ydev))
        ga(kind, 1, blk(x, 1 - y, c, 2, 4), ydev).wait_recv()
        start(ga(kind, 3, blk(x, 1 - y, c, 2, 4), xdev))
        ga(kind, 4, blk(1 - x, y, c, 2, 4), xdev).wait_recv()
        start(co(kind, 1, blk(1 - x, y, c, 0, 4)))
        ga(kind, 5, blk(x, 1 - y, c, 0, 2), ydev).wait_recv()
        start(co(kind, 2, blk(x, 1 - y, c, 0, 4)))

    def gend(kind, blk):
        ga(kind, 2, blk(1 - x, 1 - y, c, 0, 2), ydev).wait_recv()
        start(co(kind, 3, blk(1 - x, 1 - y, c, 0, 2)))
        ga(kind, 3, blk(1 - x, 1 - y, c, 2, 4), xdev).wait_recv()
        start(co(kind, 4, blk(1 - x, 1 - y, c, 2, 4)))
        co(kind, 0, blk(x, y, 1 - c, 0, 4)).wait_recv()
        co(kind, 1, blk(1 - x, y, 1 - c, 0, 4)).wait_recv()
        co(kind, 2, blk(x, 1 - y, 1 - c, 0, 4)).wait_recv()
        co(kind, 3, blk(1 - x, 1 - y, 1 - c, 0, 2)).wait_recv()
        co(kind, 4, blk(1 - x, 1 - y, 1 - c, 2, 4)).wait_recv()

    def inter(ref):
        return lambda xx, yy, cc, a, b: ref.at[pl.ds(a, b - a), xx, :, cols(yy, cc)]

    def halves(ref):
        def blk(xx, yy, cc, a, b):
            if b - a == 4:
                return ref.at[pl.ds(2 * xx, 2), :, :, cols(yy, cc)]
            return ref.at[2 * xx + a // 2, :, :, cols(yy, cc)]

        return blk

    def bstart(kind, ref, part):
        start(ga(kind, 0, ref.at[:, x, :, mycols], xdev))
        start(ga(kind, 1, part(ref, 1 - y, x, y, c), ydev))
        start(co(kind, 0, part(ref, y, x, y, c)))

    def bx(kind, ref, part):
        ga(kind, 0, ref.at[:, 1 - x, :, mycols], xdev).wait_recv()
        start(ga(kind, 2, part(ref, 1 - y, 1 - x, y, c), ydev))
        start(co(kind, 1, part(ref, y, 1 - x, y, c)))

    def bc(kind, ref, part):
        ga(kind, 1, part(ref, y, x, 1 - y, c), ydev).wait_recv()
        start(co(kind, 2, part(ref, y, x, 1 - y, c)))
        ga(kind, 2, part(ref, y, 1 - x, 1 - y, c), ydev).wait_recv()
        start(co(kind, 3, part(ref, y, 1 - x, 1 - y, c)))

    def bend(kind, ref, part):
        for n, (xx, yy) in enumerate(((x, y), (1 - x, y), (x, 1 - y), (1 - x, 1 - y))):
            co(kind, n, part(ref, y, xx, yy, 1 - c)).wait_recv()

    def allrows(ref, to_y, xx, yy, cc):
        return ref.at[:, xx, :, cols(yy, cc)]

    def tworows(ref, to_y, xx, yy, cc):
        return ref.at[pl.ds(2 * to_y, 2), xx, :, cols(yy, cc)]

    def rstart(kind, rowref):
        b = rowref(y, c)
        start(ga(kind, 0, b, ydev))
        start(co(kind, 0, b))

    def rmid(kind, rowref):
        ga(kind, 0, rowref(1 - y, c), ydev).wait_recv()
        start(co(kind, 1, rowref(1 - y, c)))

    def rend(kind, rowref):
        co(kind, 0, rowref(y, 1 - c)).wait_recv()
        co(kind, 1, rowref(1 - y, 1 - c)).wait_recv()

    def srows(ref):
        return lambda yy, cc: ref.at[:, :, cols(yy, cc)]

    def xrows(ref):
        return lambda yy, cc: ref.at[:, x, :, cols(yy, cc)]

    barrier = pltpu.get_barrier_semaphore()
    peers = [(lax.rem(dp + j, 8), q) for j in range(1, 8)]
    peers += [at(z, x, 1 - y, c), at(z, 1 - x, 1 - y, c), at(z, x, y, 1 - c)]
    for peer in peers:
        pl.semaphore_signal(barrier, inc=1, device_id=peer, device_id_type=MESH)

    loads = {}
    for n, (src, dst) in enumerate((
        (feat_hbm, feat_ref), (og_hbm, og_ref), (lb_hbm, lb_ref), (rb_hbm, rb_ref),
        (m1_hbm, m1_ref), (m2_hbm, m2_ref), (sl_hbm, sl_ref), (sr_hbm, sr_ref),
    )):
        loads[n] = pltpu.make_async_copy(src, dst, in_sem.at[n])
        loads[n].start()
    pack_ref[0:16] = ng_ref[...]
    pack_ref[16:18] = nmi_ref[...]
    pack_ref[18:20] = nvi_ref[...]
    pack_ref[20:24] = jnp.zeros((4, 128), F32)
    norm_all[dp] = pack_ref[...]
    loads[0].wait()
    ft[...] = feat_ref[:, pl.ds(pl.multiple_of((1 - x) * half, half), half)].T
    loads[1].wait()

    def tile_of(k):
        zz = jnp.minimum(z, 3 - z)
        base = (3, 2, 1 - zz, zz)[k]
        return jnp.where(z < 2, base, 3 - base)

    def og(t):
        return og_ref[:, pl.ds(pl.multiple_of(t * width, width), width)]

    def partial(k):
        t = tile_of(k)
        ppart[t] = dot(ft[...], og(t), 1, 0).astype(BF)

    def xsend(k):
        t = tile_of(k)
        start(remote(ppart.at[t], xrecv.at[t], x_send.at[t], x_recv.at[t], xdev))

    partial(0)
    loads[2].wait()
    loads[3].wait()
    zl[...] = lb_ref[...].astype(BF)
    zr[...] = rb_ref[...].astype(BF)
    L[z, x, :, mycols] = zl[z]
    R[z, x, :, mycols] = zr[z]
    pl.semaphore_wait(barrier, len(peers))

    def tile_in(src, dst):
        return (lambda zz: src.at[zz]), dst

    lz = tile_in(zl, lambda s: L.at[s, x, :, mycols])
    rz = tile_in(zr, lambda s: R.at[s, x, :, mycols])
    xsend(0)
    zspread(0, *lz)
    zspread(1, *rz)
    partial(1)
    xsend(1)
    partial(2)
    partial(3)
    for j in range(1, 8):
        dd = lax.rem(dp + j, 8)
        start(remote(pack_ref, norm_all.at[dp], nm_send.at[j], nm_recv.at[dp], (dd, q)))
    ft[...] = feat_ref[:, pl.ds(pl.multiple_of(x * half, half), half)].T
    for k in range(4):
        t = tile_of(k)
        own[t] = dot(ft[...], og(t), 1, 0)
    for n in range(4, 8):
        loads[n].wait()
    zsl[...] = sl_ref[...].astype(BF)
    zsr[...] = sr_ref[...].astype(BF)
    zm1[...] = m1_ref[...].astype(BF)
    zm2[...] = m2_ref[...].astype(BF)
    SL[z, :, mycols] = zsl[z]
    SR[z, :, mycols] = zsr[z]
    m1t[z] = zm1[z]
    m2t[z] = zm2[z]

    def xwait(t):
        remote(ppart.at[t], xrecv.at[t], x_send.at[t], x_recv.at[t], at(z, 1 - x, y, c)).wait_recv()

    def lwait(d, t):
        remote(lsend.at[t], line.at[d, t], ln_send.at[t], ln_recv.at[d, t], at(z, x, y, 1 - c)).wait_recv()

    slz = tile_in(zsl, lambda s: SL.at[s, :, mycols])
    srz = tile_in(zsr, lambda s: SR.at[s, :, mycols])
    m1z = tile_in(zm1, lambda s: m1t.at[s])
    m2z = tile_in(zm2, lambda s: m2t.at[s])

    def hop(k):
        t = tile_of(k)
        right = t > z
        d = jnp.where(right, 0, 1)
        zn = jnp.where(right, z + 1, z - 1)
        inner_hop = jnp.where(right, z > 0, z < 3)
        xwait(t)
        own[t] += xrecv[t].astype(F32)

        @pl.when(inner_hop)
        def _():
            lwait(d, t)
            lsend[t] = (own[t] + line[d, t].astype(F32)).astype(BF)

        @pl.when(jnp.logical_not(inner_hop))
        def _():
            lsend[t] = own[t].astype(BF)

        start(remote(lsend.at[t], line.at[d, t], ln_send.at[t], ln_recv.at[d, t], at(zn, x, y, c)))

    zwait(0, *lz)
    bstart(0, L, allrows)
    xsend(2)
    hop(0)
    zwait(1, *rz)
    bstart(1, R, tworows)
    xsend(3)
    hop(1)
    bx(0, L, allrows)
    hop(2)
    zspread(2, *slz)
    zspread(3, *srz)
    zspread(4, *m1z)
    zspread(5, *m2z)
    bx(1, R, tworows)
    bc(0, L, allrows)
    xwait(z)
    own[z] += xrecv[z].astype(F32)

    @pl.when(z > 0)
    def _():
        lwait(0, z)
        own[z] += line[0, z].astype(F32)

    @pl.when(z < 3)
    def _():
        lwait(1, z)
        own[z] += line[1, z].astype(F32)

    G[pl.ds(2 * x, 2), :, :, mycols] = own[z].astype(BF).reshape(2, 2, slab, width)
    gstart(2, halves(G))
    gmid(2, halves(G))
    zwait(2, *slz)
    rstart(6, srows(SL))
    zwait(3, *srz)
    rstart(7, srows(SR))
    bc(1, R, tworows)
    bend(0, L, allrows)
    bend(1, R, tworows)
    gend(2, halves(G))
    zwait(4, *m1z)
    zwait(5, *m2z)

    def full(ref):
        return ref[...].reshape(8 * slab, 8 * slab)

    def rows(ref):
        return ref[:, x].reshape(half, 8 * slab)

    def colb(ref):
        return ref[:, :, :, mycols].reshape(8 * slab, width)

    def lane(ref, zz):
        return ref[:, :, :, pl.ds(pl.multiple_of((2 * zz + x) * slab, slab), slab)].reshape(8 * slab, slab)

    inner = dot(full(G), colb(R), 1, 0).astype(BF)
    for s in range(4):
        rotated = dot(lane(L, s), inner, 0, 0)
        rot_s[s] = rotated.astype(BF)
        one = 0.9 * m1t[s].astype(F32) + 0.1 * rotated
        two = 0.95 * m2t[s].astype(F32) + 0.05 * rotated * rotated
        DIR[s, x, :, mycols] = (one / FIX_ONE / (jnp.sqrt(two / FIX_TWO) + 1e-08)).astype(BF)
    gstart(3, inter(DIR))
    rot_home[z] = rot_s[z]
    rotz = tile_in(rot_s, lambda s: rot_home.at[s])
    zspread(6, *rotz)

    def power(prods, stat, basis, prod, slot):
        prods[...] = prod.astype(BF)
        stats = (0.95 * stat[...].astype(F32) + 0.05 * prods[...].astype(F32)).astype(BF)
        out = dot(stats.reshape(half, 8 * slab), colb(basis), 1, 0)
        total = jnp.sum(out * out, axis=0, keepdims=True)
        sq[0, slot] = jnp.broadcast_to(total, (8, width))
        start(remote(sq.at[0, slot], sq.at[1, slot], sq_send.at[slot], sq_recv.at[slot], at(z, 1 - x, y, c)))
        return out

    def iterate(out, slot, it):
        remote(sq.at[0, slot], sq.at[1, slot], sq_send.at[slot], sq_recv.at[slot], at(z, 1 - x, y, c)).wait_recv()
        total = (sq[0, slot] + sq[1, slot])[0:1]
        it[:, x, :, mycols] = (out * lax.rsqrt(total + 1e-06)).astype(BF).reshape(4, slab, width)

    rmid(6, srows(SL))
    prod_l = dot(rows(G), full(G), 1, 1).reshape(4, slab, 8 * slab)
    rend(6, srows(SL))
    pow_l = power(PL, SL, L, prod_l, 0)
    pl_home[z] = PL[z, :, mycols]
    plz = (lambda zz: PL.at[zz, :, mycols]), (lambda s: pl_home.at[s])
    zspread(7, *plz)
    rmid(7, srows(SR))
    for s in range(4):
        PR[s] = dot(lane(G, s), full(G), 0, 0).astype(BF)
    rend(7, srows(SR))
    pow_r = power(PR, SR, R, PR[...], 1)
    pr_home[z] = PR[z, :, mycols]
    prz = (lambda zz: PR.at[zz, :, mycols]), (lambda s: pr_home.at[s])
    zspread(8, *prz)
    iterate(pow_l, 0, IL)
    gmid(3, inter(DIR))
    gstart(4, inter(IL))
    iterate(pow_r, 1, IR)
    gstart(5, inter(IR))

    gend(3, inter(DIR))
    back = dot(full(DIR), R[q].reshape(2 * slab, 8 * slab), 1, 1).astype(BF)
    upd[z] = dot(rows(L), back, 1, 0).astype(BF).reshape(4, slab, width)

    def ucopy(t, h, right):
        zn = jnp.clip(z + 1 if right else z - 1, 0, 3)
        part = upd.at[t, h]
        return remote(part, part, (up_r if right else up_l).at[t, h], up_recv.at[t, h], at(zn, x, y, c))

    def upd_on(t, h, right):
        @pl.when(z < 3 if right else z > 0)
        def _():
            ucopy(t, h, right).start()

    for h in range(4):
        upd_on(z, h, True)
        upd_on(z, h, False)
    gmid(4, inter(IL))

    def refine(it, kind, out_s, home, zk):
        gend(kind, inter(it))
        gram = dot(rows(it), full(it), 1, 1).astype(BF)
        mine = it[:, x, :, mycols].reshape(half, width).astype(F32)
        new = 1.5 * mine - 0.5 * dot(gram, colb(it), 1, 0)
        out_s[...] = new.astype(BF).reshape(4, slab, width)
        home[z] = out_s[z]
        mv = tile_in(out_s, lambda s: home.at[s])
        return mv

    def relay(j, h):
        @pl.when(z - j >= 0)
        def _():
            t = jnp.maximum(z - j, 0)
            ucopy(t, h, True).wait_recv()
            upd_on(t, h, True)

        @pl.when(z + j <= 3)
        def _():
            t = jnp.minimum(z + j, 3)
            ucopy(t, h, False).wait_recv()
            upd_on(t, h, False)

    gmid(5, inter(IR))
    for h in range(4):
        relay(1, h)
    nlz = refine(IL, 4, nl_s, nl_home, 9)
    edge = jnp.logical_or(z == 0, z == 3)
    inside = jnp.logical_not(edge)
    zspread_if(edge, 9, *nlz)
    for h in range(4):
        relay(2, h)
    nrz = refine(IR, 5, nr_s, nr_home, 10)
    zspread_if(edge, 10, *nrz)

    def pick(who, h):
        got = jnp.zeros((slab, width), BF)
        for t in range(4):
            got = jnp.where(own_ref[t] == who, upd[t, h], got)
        return got

    def ucross(h, to):
        return remote(
            upd_px.at[h], upd_out.at[h, to], ux_sem.at[h], ux_sem.at[4 + h], xdev
        )

    for h in range(4):
        relay(3, h)
        upd_px[h] = pick(z * 2 + 1 - x, h)
        start(ucross(h, x))
    zspread_if(inside, 9, *nlz)
    zspread_if(inside, 10, *nrz)
    for h in range(4):
        upd_out[h, x] = pick(dp, h)
    for j in range(1, 8):
        dd = lax.rem(dp + j, 8)
        remote(pack_ref, norm_all.at[dd], nm_send.at[j], nm_recv.at[dd], (dd, q)).wait_recv()
    for j in range(8):
        nscr[0, 2 * j : 2 * j + 2] = norm_all[j, 16:18]
        nscr[1, 2 * j : 2 * j + 2] = norm_all[j, 18:20]
    total = jnp.sum(norm_all[:, 0:16], axis=0)
    nm = 0.9 * nscr[0] + 0.1 * total
    nv = 0.95 * nscr[1] + 0.05 * total * total
    step = nm / FIX_ONE / (jnp.sqrt(nv / FIX_TWO) + 1e-08)
    ns_out[...] = jnp.where(own_ref[nt] == dp, step, jnp.zeros_like(step))
    nscr[0] = nm
    nscr[1] = nv
    nm_out[...] = nscr[0, pl.ds(2 * dp, 2)]
    nv_out[...] = nscr[1, pl.ds(2 * dp, 2)]
    zwait(6, *rotz)
    zwait(7, *plz)
    zwait(8, *prz)
    zwait(9, *nlz)
    zwait(10, *nrz)
    for h in range(4):
        ucross(h, 1 - x).wait_recv()

    @pl.when(z < 3)
    def _():
        for j in range(4):
            @pl.when(z - j >= 0)
            def _():
                for h in range(4):
                    ucopy(jnp.maximum(z - j, 0), h, True).wait_send()

    @pl.when(z > 0)
    def _():
        for j in range(4):
            @pl.when(z + j <= 3)
            def _():
                for h in range(4):
                    ucopy(jnp.minimum(z + j, 3), h, False).wait_send()

    zsent(9, *nlz)
    zsent(10, *nrz)
    for cp in pending:
        cp.wait_send()


def finish_kernel(
    m1, m2, sl, sr, rot, prod_l, prod_r, new_l, new_r, slot, nm, nv, ns,
    m1_out, m2_out, sl_out, sr_out, bl_out, br_out, slot_out, nm_out, nv_out, ns_out,
):
    turned = rot[...].astype(F32)
    m1_out[...] = 0.9 * m1[...] + 0.1 * turned
    m2_out[...] = 0.95 * m2[...] + 0.05 * turned * turned
    sl_out[...] = 0.95 * sl[...] + 0.05 * prod_l[...].astype(F32)
    sr_out[...] = 0.95 * sr[...] + 0.05 * prod_r[...].astype(F32)
    bl_out[...] = new_l[...].astype(F32)
    br_out[...] = new_r[...].astype(F32)
    slot_out[...] = slot[...]
    nm_out[...] = nm[...]
    nv_out[...] = nv[...]
    ns_out[...] = ns[...]


def fused_shards(
    features,
    out_grads,
    norm_grads,
    owners,
    moment1,
    moment2,
    left_stats,
    right_stats,
    left_basis,
    right_basis,
    norm_m,
    norm_v,
):
    nt, slab, width = moment1.shape
    full = 8 * slab
    flat = out_grads.reshape(out_grads.shape[0], nt * width)
    vm = pl.BlockSpec(memory_space=pltpu.VMEM)
    hbm = pl.BlockSpec(memory_space=pl.ANY)
    home = jax.ShapeDtypeStruct((nt, slab, width), BF)
    big = pltpu.VMEM((4, 2, slab, full), BF)
    blk = pltpu.VMEM((4, slab, width), BF)
    piece = (4 * slab, width)
    dma = pltpu.SemaphoreType.DMA
    rot, prod_l, prod_r, new_l, new_r, slot, nm, nv, ns = pl.pallas_call(
        fused_kernel,
        out_shape=[home] * 5
        + [
            jax.ShapeDtypeStruct((4, 2, slab, width), BF),
            jax.ShapeDtypeStruct((2, 128), F32),
            jax.ShapeDtypeStruct((2, 128), F32),
            jax.ShapeDtypeStruct((16, 128), F32),
        ],
        in_specs=[hbm] * 2 + [vm] * 3 + [pl.BlockSpec(memory_space=pltpu.SMEM)] + [hbm] * 6,
        out_specs=[vm] * 9,
        scratch_shapes=[
            pltpu.VMEM(features.shape, BF),
            pltpu.VMEM(flat.shape, BF),
        ]
        + [pltpu.VMEM((nt, slab, width), F32)] * 6
        + [pltpu.VMEM((24, 128), F32), dma((8,))]
        + [
            pltpu.VMEM((4 * slab, features.shape[0]), BF),
            pltpu.VMEM((4,) + piece, BF),
            pltpu.VMEM((4,) + piece, F32),
            pltpu.VMEM((4,) + piece, BF),
            pltpu.VMEM((2, 4) + piece, BF),
            pltpu.VMEM((4,) + piece, BF),
        ]
        + [blk] * 6
        + [big] * 6
        + [pltpu.VMEM((4, slab, full), BF)] * 4
        + [blk] * 5
        + [pltpu.VMEM((4, 4, slab, width), BF), blk, pltpu.VMEM((2, 2, 8, width), F32)]
        + [
            dma((11, 4)), dma((11, 4)), dma((4,)), dma((4,)), dma((4,)), dma((2, 4)),
            dma((8, 6)), dma((8, 6)), dma((8, 5)), dma((8, 5)),
        ]
        + [pltpu.VMEM((8, 24, 128), F32), pltpu.VMEM((2, 16, 128), F32)]
        + [dma((4, 4)), dma((4, 4)), dma((4, 4)), dma((8,)), dma((8,)), dma((8,)), dma((2,)), dma((2,))],
        compiler_params=pltpu.CompilerParams(
            collective_id=0, has_side_effects=True, vmem_limit_bytes=56 * 2**20
        ),
        cost_estimate=pl.CostEstimate(flops=10**10, bytes_accessed=2**24, transcendentals=0),
    )(
        features, flat, norm_grads.reshape(16, 128), norm_m.reshape(2, 128), norm_v.reshape(2, 128), owners,
        moment1, moment2, left_stats, right_stats, left_basis, right_basis,
    )
    tile = pl.BlockSpec((2, slab, width), lambda i: (i, 0, 0))
    slots = pl.BlockSpec((2, 2, slab, width), lambda i: (i, 0, 0, 0))
    once2 = pl.BlockSpec((2, 128), lambda i: (0, 0))
    once16 = pl.BlockSpec((16, 128), lambda i: (0, 0))
    state = jax.ShapeDtypeStruct((nt, slab, width), F32)
    outs = pl.pallas_call(
        finish_kernel,
        grid=(nt // 2,),
        out_shape=[state] * 6
        + [
            jax.ShapeDtypeStruct((4, 2, slab, width), BF),
            jax.ShapeDtypeStruct((2, 128), F32),
            jax.ShapeDtypeStruct((2, 128), F32),
            jax.ShapeDtypeStruct((16, 128), F32),
        ],
        in_specs=[tile] * 9 + [slots, once2, once2, once16],
        out_specs=[tile] * 6 + [slots, once2, once2, once16],
        cost_estimate=pl.CostEstimate(flops=2**20, bytes_accessed=2**23, transcendentals=0),
    )(moment1, moment2, left_stats, right_stats, rot, prod_l, prod_r, new_l, new_r, slot, nm, nv, ns)
    slot, nm, nv, ns = outs[6:]
    return (
        *outs[:6],
        slot.reshape(1, full, width),
        nm.reshape(norm_m.shape),
        nv.reshape(norm_v.shape),
        ns.reshape(1, -1),
    )


def solution(mesh):
    in_specs = (
        P("dp", None),
        P("dp", None, "mp"),
        P("dp", None),
        P(),
        P(None, "dp", "mp"),
        P(None, "dp", "mp"),
        P(None, "dp", "mp"),
        P(None, "dp", "mp"),
        P(None, "dp", "mp"),
        P(None, "dp", "mp"),
        P("dp"),
        P("dp"),
    )
    out_specs = (
        P(None, "dp", "mp"),
        P(None, "dp", "mp"),
        P(None, "dp", "mp"),
        P(None, "dp", "mp"),
        P(None, "dp", "mp"),
        P(None, "dp", "mp"),
        P("dp", None, "mp"),
        P("dp"),
        P("dp"),
        P("dp", None),
    )
    fused = mesh.shape["dp"] == 8 and mesh.shape["mp"] == 4
    body = fused_shards if fused else shards
    return jax.shard_map(body, mesh=mesh, in_specs=in_specs, out_specs=out_specs, check_vma=False)
```

```python
import jax
import jax.numpy as jnp
from jax import lax
from jax.experimental import pallas as pl
from jax.experimental.pallas import tpu as pltpu
from jax.sharding import PartitionSpec as P

MESH = pl.DeviceIdType.MESH

FIX_ONE = 1.0 - 0.9**10
FIX_TWO = 1.0 - 0.95**10
BF = jnp.bfloat16
F32 = jnp.float32


def dot(left, right, left_dim, right_dim):
    return lax.dot_general(
        left, right, (((left_dim,), (right_dim,)), ((), ())), preferred_element_type=F32
    )


contract = dot


def to_tile(blocks):
    out = lax.all_to_all(blocks, "mp", split_axis=1, concat_axis=1, tiled=True)
    k, n, r, c = out.shape
    return out.transpose(0, 2, 1, 3).reshape(k, r, n * c)


def to_home(rows, n):
    k, r, c = rows.shape
    out = rows.reshape(k, r, n, c // n).transpose(0, 2, 1, 3)
    return lax.all_to_all(out, "mp", split_axis=1, concat_axis=1, tiled=True)


def gather_rows(rows):
    return lax.all_gather(rows, "dp", axis=0, tiled=True)


def normalize(power):
    wide = power.astype(F32)
    return lax.rsqrt(jnp.sum(wide * wide, axis=0, keepdims=True) + 1e-06)


def shards(
    features,
    out_grads,
    norm_grads,
    owners,
    moment1,
    moment2,
    left_stats,
    right_stats,
    left_basis,
    right_basis,
    norm_m,
    norm_v,
):
    dp = lax.axis_size("dp")
    tiles, slab, width = moment1.shape
    full = slab * dp
    me = lax.axis_index("dp")
    row0 = me * slab

    narrow = to_tile(jnp.stack([left_basis, right_basis, left_stats, right_stats]).astype(BF))
    left_full = gather_rows(narrow[0])
    right_full = gather_rows(narrow[1])

    flat = out_grads.reshape(out_grads.shape[0], tiles * width)
    partial = contract(features, flat, 0, 0).astype(BF).reshape(dp, slab, tiles * width)
    parts = lax.all_to_all(partial, "dp", split_axis=0, concat_axis=0, tiled=True)
    grad_home = jnp.sum(parts.astype(F32), axis=0).astype(BF)
    grad_home = grad_home.reshape(slab, tiles, width).transpose(1, 0, 2)
    grad_rows = to_tile(grad_home[None])[0]
    grad_full = gather_rows(grad_rows)

    wide = to_tile(jnp.stack([moment1, moment2]))

    prod_l = contract(grad_rows, grad_full, 1, 1)
    grad_cols = lax.dynamic_slice_in_dim(grad_full, row0, slab, 1)
    prod_r = contract(grad_cols, grad_full, 0, 0)
    stats_l = (0.95 * narrow[2].astype(F32) + 0.05 * prod_l).astype(BF)
    stats_r = (0.95 * narrow[3].astype(F32) + 0.05 * prod_r).astype(BF)
    power_l = contract(stats_l, left_full, 1, 0).astype(BF)
    power_r = contract(stats_r, right_full, 1, 0).astype(BF)
    power_l_full = gather_rows(power_l)
    power_r_full = gather_rows(power_r)

    left_cols = lax.dynamic_slice_in_dim(left_full, row0, slab, 1)
    half = contract(left_cols, grad_full, 0, 0).astype(BF)
    rotated = contract(half, right_full, 1, 0)
    tile_one = 0.9 * wide[0] + 0.1 * rotated
    tile_two = 0.95 * wide[1] + 0.05 * rotated * rotated
    direction = (tile_one / FIX_ONE / (jnp.sqrt(tile_two / FIX_TWO) + 1e-08)).astype(BF)
    back = contract(direction, right_full, 1, 1).astype(BF)
    back_full = gather_rows(back)

    home1 = to_home(jnp.stack([rotated, prod_l, prod_r]).astype(BF), tiles).astype(F32)
    new_one = 0.9 * moment1 + 0.1 * home1[0]
    new_two = 0.95 * moment2 + 0.05 * home1[0] * home1[0]
    new_sl = 0.95 * left_stats + 0.05 * home1[1]
    new_sr = 0.95 * right_stats + 0.05 * home1[2]

    update = contract(narrow[0], back_full, 1, 0).astype(BF)

    def refine(power_full, power_rows):
        scale = normalize(power_full)
        iter_full = (power_full.astype(F32) * scale).astype(BF)
        iter_rows = (power_rows.astype(F32) * scale).astype(BF)
        gram = contract(iter_rows, iter_full, 1, 1).astype(BF)
        return 1.5 * iter_rows.astype(F32) - 0.5 * contract(gram, iter_full, 1, 0)

    new_l = refine(power_l_full, power_l)
    new_r = refine(power_r_full, power_r)
    home2 = to_home(jnp.stack([new_l.astype(BF), new_r.astype(BF), update]), tiles)
    new_bl = home2[0].astype(F32)
    new_br = home2[1].astype(F32)
    slot_of = jnp.arange(dp, dtype=jnp.int32)[:, None, None]
    slots = jnp.zeros((dp, slab, width), BF)
    for n in range(tiles):
        slots = jnp.where(slot_of == owners[n], home2[2, n][None], slots)
    update_slot = lax.all_to_all(slots, "dp", split_axis=0, concat_axis=0, tiled=True)
    update_slot = update_slot.reshape(1, full, width)

    norm_parts = norm_grads.reshape(dp, norm_m.shape[0])
    norm_parts = lax.all_to_all(norm_parts, "dp", split_axis=0, concat_axis=0, tiled=True)
    norm_total = jnp.sum(norm_parts, axis=0)
    new_nm = 0.9 * norm_m + 0.1 * norm_total
    new_nv = 0.95 * norm_v + 0.05 * norm_total * norm_total
    norm_step = new_nm / FIX_ONE / (jnp.sqrt(new_nv / FIX_TWO) + 1e-08)
    to_owner = (jnp.arange(dp, dtype=jnp.int32) == owners[tiles])[:, None]
    norm_out = jnp.where(to_owner, norm_step[None], 0.0)
    norm_slot = lax.all_to_all(norm_out, "dp", split_axis=0, concat_axis=0, tiled=True)
    norm_slot = norm_slot.reshape(1, -1)
    return (
        new_one,
        new_two,
        new_sl,
        new_sr,
        new_bl,
        new_br,
        update_slot,
        new_nm,
        new_nv,
        norm_slot,
    )


def fused_kernel(
    feat_hbm, og_hbm, ng_ref, nmi_ref, nvi_ref, own_ref, m1_hbm, m2_hbm, sl_hbm, sr_hbm, lb_hbm, rb_hbm,
    rot_home, pl_home, pr_home, nl_home, nr_home, upd_out, nm_out, nv_out, ns_out,
    feat_ref, og_ref, m1_ref, m2_ref, sl_ref, sr_ref, lb_ref, rb_ref, pack_ref, in_sem,
    ft, ppart, own, xrecv, line, lsend,
    zl, zr, zsl, zsr, zm1, zm2,
    L, R, G, DIR, IL, IR, SL, SR, PL, PR, m1t, m2t, rot_s, nl_s, nr_s, upd, upd_px, sq,
    zs_send, zs_recv, x_send, x_recv, ln_send, ln_recv, ga_send, ga_recv, co_send, co_recv,
    norm_all, nscr, up_r, up_l, up_recv, ux_sem, nm_send, nm_recv, sq_send, sq_recv,
):
    nt, slab, width = m1_ref.shape
    dp = lax.axis_index("dp")
    q = lax.axis_index("mp")
    z, x = dp // 2, lax.rem(dp, 2)
    y, c = q // 2, lax.rem(q, 2)
    half = 4 * slab

    def at(zz, xx, yy, cc):
        return (zz * 2 + xx, yy * 2 + cc)

    def cols(yy, cc):
        return pl.ds(pl.multiple_of((yy * 2 + cc) * width, width), width)

    mycols = cols(y, c)

    def remote(src, dst, ssem, rsem, dev):
        return pltpu.make_async_remote_copy(
            src_ref=src, dst_ref=dst, send_sem=ssem, recv_sem=rsem, device_id=dev, device_id_type=MESH
        )

    pending = []

    def start(cp):
        cp.start()
        pending.append(cp)

    def zspread(kind, src, dst):
        for j in (1, 2, 3):
            zz = lax.rem(z + j, 4)
            start(remote(src(zz), dst(z), zs_send.at[kind, j], zs_recv.at[kind, z], at(zz, x, y, c)))

    def zwait(kind, src, dst):
        for j in (1, 2, 3):
            zz = lax.rem(z + j, 4)
            remote(src(zz), dst(zz), zs_send.at[kind, j], zs_recv.at[kind, zz], at(zz, x, y, c)).wait_recv()

    def zspread_if(cond, kind, src, dst):
        @pl.when(cond)
        def _():
            for j in (1, 2, 3):
                zz = lax.rem(z + j, 4)
                remote(src(zz), dst(z), zs_send.at[kind, j], zs_recv.at[kind, z], at(zz, x, y, c)).start()

    def zsent(kind, src, dst):
        for j in (1, 2, 3):
            zz = lax.rem(z + j, 4)
            remote(src(zz), dst(z), zs_send.at[kind, j], zs_recv.at[kind, z], at(zz, x, y, c)).wait_send()

    xdev, ydev, cdev = at(z, 1 - x, y, c), at(z, x, 1 - y, c), at(z, x, y, 1 - c)

    def ga(kind, slot, ref, dev):
        return remote(ref, ref, ga_send.at[kind, slot], ga_recv.at[kind, slot], dev)

    def co(kind, slot, ref):
        return remote(ref, ref, co_send.at[kind, slot], co_recv.at[kind, slot], cdev)

    def gstart(kind, blk):
        start(ga(kind, 0, blk(x, y, c, 0, 2), xdev))
        start(ga(kind, 1, blk(x, y, c, 2, 4), ydev))
        start(ga(kind, 4, blk(x, y, c, 2, 4), xdev))
        start(ga(kind, 5, blk(x, y, c, 0, 2), ydev))
        start(co(kind, 0, blk(x, y, c, 0, 4)))

    def gmid(kind, blk):
        ga(kind, 0, blk(1 - x, y, c, 0, 2), xdev).wait_recv()
        start(ga(kind, 2, blk(1 - x, y, c, 0, 2), ydev))
        ga(kind, 1, blk(x, 1 - y, c, 2, 4), ydev).wait_recv()
        start(ga(kind, 3, blk(x, 1 - y, c, 2, 4), xdev))
        ga(kind, 4, blk(1 - x, y, c, 2, 4), xdev).wait_recv()
        start(co(kind, 1, blk(1 - x, y, c, 0, 4)))
        ga(kind, 5, blk(x, 1 - y, c, 0, 2), ydev).wait_recv()
        start(co(kind, 2, blk(x, 1 - y, c, 0, 4)))

    def gend(kind, blk):
        ga(kind, 2, blk(1 - x, 1 - y, c, 0, 2), ydev).wait_recv()
        start(co(kind, 3, blk(1 - x, 1 - y, c, 0, 2)))
        ga(kind, 3, blk(1 - x, 1 - y, c, 2, 4), xdev).wait_recv()
        start(co(kind, 4, blk(1 - x, 1 - y, c, 2, 4)))
        co(kind, 0, blk(x, y, 1 - c, 0, 4)).wait_recv()
        co(kind, 1, blk(1 - x, y, 1 - c, 0, 4)).wait_recv()
        co(kind, 2, blk(x, 1 - y, 1 - c, 0, 4)).wait_recv()
        co(kind, 3, blk(1 - x, 1 - y, 1 - c, 0, 2)).wait_recv()
        co(kind, 4, blk(1 - x, 1 - y, 1 - c, 2, 4)).wait_recv()

    def inter(ref):
        return lambda xx, yy, cc, a, b: ref.at[pl.ds(a, b - a), xx, :, cols(yy, cc)]

    def halves(ref):
        def blk(xx, yy, cc, a, b):
            if b - a == 4:
                return ref.at[pl.ds(2 * xx, 2), :, :, cols(yy, cc)]
            return ref.at[2 * xx + a // 2, :, :, cols(yy, cc)]

        return blk

    def bstart(kind, ref, part):
        start(ga(kind, 0, ref.at[:, x, :, mycols], xdev))
        start(ga(kind, 1, part(ref, 1 - y, x, y, c), ydev))
        start(co(kind, 0, part(ref, y, x, y, c)))

    def bx(kind, ref, part):
        ga(kind, 0, ref.at[:, 1 - x, :, mycols], xdev).wait_recv()
        start(ga(kind, 2, part(ref, 1 - y, 1 - x, y, c), ydev))
        start(co(kind, 1, part(ref, y, 1 - x, y, c)))

    def bc(kind, ref, part):
        ga(kind, 1, part(ref, y, x, 1 - y, c), ydev).wait_recv()
        start(co(kind, 2, part(ref, y, x, 1 - y, c)))
        ga(kind, 2, part(ref, y, 1 - x, 1 - y, c), ydev).wait_recv()
        start(co(kind, 3, part(ref, y, 1 - x, 1 - y, c)))

    def bend(kind, ref, part):
        for n, (xx, yy) in enumerate(((x, y), (1 - x, y), (x, 1 - y), (1 - x, 1 - y))):
            co(kind, n, part(ref, y, xx, yy, 1 - c)).wait_recv()

    def allrows(ref, to_y, xx, yy, cc):
        return ref.at[:, xx, :, cols(yy, cc)]

    def tworows(ref, to_y, xx, yy, cc):
        return ref.at[pl.ds(2 * to_y, 2), xx, :, cols(yy, cc)]

    def rstart(kind, rowref):
        b = rowref(y, c)
        start(ga(kind, 0, b, ydev))
        start(co(kind, 0, b))

    def rmid(kind, rowref):
        ga(kind, 0, rowref(1 - y, c), ydev).wait_recv()
        start(co(kind, 1, rowref(1 - y, c)))

    def rend(kind, rowref):
        co(kind, 0, rowref(y, 1 - c)).wait_recv()
        co(kind, 1, rowref(1 - y, 1 - c)).wait_recv()

    def srows(ref):
        return lambda yy, cc: ref.at[:, :, cols(yy, cc)]

    def xrows(ref):
        return lambda yy, cc: ref.at[:, x, :, cols(yy, cc)]

    barrier = pltpu.get_barrier_semaphore()
    peers = [(lax.rem(dp + j, 8), q) for j in range(1, 8)]
    peers += [at(z, x, 1 - y, c), at(z, 1 - x, 1 - y, c), at(z, x, y, 1 - c)]
    for peer in peers:
        pl.semaphore_signal(barrier, inc=1, device_id=peer, device_id_type=MESH)

    loads = {}
    for n, (src, dst) in enumerate((
        (feat_hbm, feat_ref), (og_hbm, og_ref), (lb_hbm, lb_ref), (rb_hbm, rb_ref),
        (m1_hbm, m1_ref), (m2_hbm, m2_ref), (sl_hbm, sl_ref), (sr_hbm, sr_ref),
    )):
        loads[n] = pltpu.make_async_copy(src, dst, in_sem.at[n])
        loads[n].start()
    pack_ref[0:16] = ng_ref[...]
    pack_ref[16:18] = nmi_ref[...]
    pack_ref[18:20] = nvi_ref[...]
    pack_ref[20:24] = jnp.zeros((4, 128), F32)
    norm_all[dp] = pack_ref[...]
    loads[0].wait()
    ft[...] = feat_ref[:, pl.ds(pl.multiple_of((1 - x) * half, half), half)].T
    loads[1].wait()

    def tile_of(k):
        zz = jnp.minimum(z, 3 - z)
        base = (3, 2, 1 - zz, zz)[k]
        return jnp.where(z < 2, base, 3 - base)

    def og(t):
        return og_ref[:, pl.ds(pl.multiple_of(t * width, width), width)]

    def partial(k):
        t = tile_of(k)
        ppart[t] = dot(ft[...], og(t), 1, 0).astype(BF)

    def xsend(k):
        t = tile_of(k)
        start(remote(ppart.at[t], xrecv.at[t], x_send.at[t], x_recv.at[t], xdev))

    partial(0)
    loads[2].wait()
    loads[3].wait()
    zl[...] = lb_ref[...].astype(BF)
    zr[...] = rb_ref[...].astype(BF)
    L[z, x, :, mycols] = zl[z]
    R[z, x, :, mycols] = zr[z]
    pl.semaphore_wait(barrier, len(peers))

    def tile_in(src, dst):
        return (lambda zz: src.at[zz]), dst

    lz = tile_in(zl, lambda s: L.at[s, x, :, mycols])
    rz = tile_in(zr, lambda s: R.at[s, x, :, mycols])
    xsend(0)
    zspread(0, *lz)
    zspread(1, *rz)
    partial(1)
    xsend(1)
    partial(2)
    partial(3)
    for j in range(1, 8):
        dd = lax.rem(dp + j, 8)
        start(remote(pack_ref, norm_all.at[dp], nm_send.at[j], nm_recv.at[dp], (dd, q)))
    ft[...] = feat_ref[:, pl.ds(pl.multiple_of(x * half, half), half)].T
    for k in range(4):
        t = tile_of(k)
        own[t] = dot(ft[...], og(t), 1, 0)
    for n in range(4, 8):
        loads[n].wait()
    zsl[...] = sl_ref[...].astype(BF)
    zsr[...] = sr_ref[...].astype(BF)
    zm1[...] = m1_ref[...].astype(BF)
    zm2[...] = m2_ref[...].astype(BF)
    SL[z, :, mycols] = zsl[z]
    SR[z, :, mycols] = zsr[z]
    m1t[z] = zm1[z]
    m2t[z] = zm2[z]

    def xwait(t):
        remote(ppart.at[t], xrecv.at[t], x_send.at[t], x_recv.at[t], at(z, 1 - x, y, c)).wait_recv()

    def lwait(d, t):
        remote(lsend.at[t], line.at[d, t], ln_send.at[t], ln_recv.at[d, t], at(z, x, y, 1 - c)).wait_recv()

    slz = tile_in(zsl, lambda s: SL.at[s, :, mycols])
    srz = tile_in(zsr, lambda s: SR.at[s, :, mycols])
    m1z = tile_in(zm1, lambda s: m1t.at[s])
    m2z = tile_in(zm2, lambda s: m2t.at[s])

    def hop(k):
        t = tile_of(k)
        right = t > z
        d = jnp.where(right, 0, 1)
        zn = jnp.where(right, z + 1, z - 1)
        inner_hop = jnp.where(right, z > 0, z < 3)
        xwait(t)
        own[t] += xrecv[t].astype(F32)

        @pl.when(inner_hop)
        def _():
            lwait(d, t)
            lsend[t] = (own[t] + line[d, t].astype(F32)).astype(BF)

        @pl.when(jnp.logical_not(inner_hop))
        def _():
            lsend[t] = own[t].astype(BF)

        start(remote(lsend.at[t], line.at[d, t], ln_send.at[t], ln_recv.at[d, t], at(zn, x, y, c)))

    zwait(0, *lz)
    bstart(0, L, allrows)
    xsend(2)
    hop(0)
    zwait(1, *rz)
    bstart(1, R, tworows)
    xsend(3)
    hop(1)
    bx(0, L, allrows)
    hop(2)
    zspread(2, *slz)
    zspread(3, *srz)
    zspread(4, *m1z)
    zspread(5, *m2z)
    bx(1, R, tworows)
    bc(0, L, allrows)
    xwait(z)
    own[z] += xrecv[z].astype(F32)

    @pl.when(z > 0)
    def _():
        lwait(0, z)
        own[z] += line[0, z].astype(F32)

    @pl.when(z < 3)
    def _():
        lwait(1, z)
        own[z] += line[1, z].astype(F32)

    G[pl.ds(2 * x, 2), :, :, mycols] = own[z].astype(BF).reshape(2, 2, slab, width)
    gstart(2, halves(G))
    gmid(2, halves(G))
    zwait(2, *slz)
    rstart(6, srows(SL))
    zwait(3, *srz)
    rstart(7, srows(SR))
    bc(1, R, tworows)
    bend(0, L, allrows)
    bend(1, R, tworows)
    gend(2, halves(G))

    def full(ref):
        return ref[...].reshape(8 * slab, 8 * slab)

    def rows(ref):
        return ref[:, x].reshape(half, 8 * slab)

    def colb(ref):
        return ref[:, :, :, mycols].reshape(8 * slab, width)

    def lane(ref, zz):
        return ref[:, :, :, pl.ds(pl.multiple_of((2 * zz + x) * slab, slab), slab)].reshape(8 * slab, slab)

    inner = dot(full(G), colb(R), 1, 0).astype(BF)
    zwait(4, *m1z)
    zwait(5, *m2z)
    for s in range(4):
        rotated = dot(lane(L, s), inner, 0, 0)
        rot_s[s] = rotated.astype(BF)
        one = 0.9 * m1t[s].astype(F32) + 0.1 * rotated
        two = 0.95 * m2t[s].astype(F32) + 0.05 * rotated * rotated
        DIR[s, x, :, mycols] = (one / FIX_ONE / (jnp.sqrt(two / FIX_TWO) + 1e-08)).astype(BF)
    gstart(3, inter(DIR))
    rot_home[z] = rot_s[z]
    rotz = tile_in(rot_s, lambda s: rot_home.at[s])
    zspread(6, *rotz)

    def power(prods, stat, basis, prod, slot):
        prods[...] = prod.astype(BF)
        stats = (0.95 * stat[...].astype(F32) + 0.05 * prods[...].astype(F32)).astype(BF)
        out = dot(stats.reshape(half, 8 * slab), colb(basis), 1, 0)
        total = jnp.sum(out * out, axis=0, keepdims=True)
        sq[0, slot] = jnp.broadcast_to(total, (8, width))
        start(remote(sq.at[0, slot], sq.at[1, slot], sq_send.at[slot], sq_recv.at[slot], at(z, 1 - x, y, c)))
        return out

    def iterate(out, slot, it):
        remote(sq.at[0, slot], sq.at[1, slot], sq_send.at[slot], sq_recv.at[slot], at(z, 1 - x, y, c)).wait_recv()
        total = (sq[0, slot] + sq[1, slot])[0:1]
        it[:, x, :, mycols] = (out * lax.rsqrt(total + 1e-06)).astype(BF).reshape(4, slab, width)

    rmid(6, srows(SL))
    prod_l = dot(rows(G), full(G), 1, 1).reshape(4, slab, 8 * slab)
    rend(6, srows(SL))
    pow_l = power(PL, SL, L, prod_l, 0)
    pl_home[z] = PL[z, :, mycols]
    plz = (lambda zz: PL.at[zz, :, mycols]), (lambda s: pl_home.at[s])
    zspread(7, *plz)
    rmid(7, srows(SR))
    for s in range(4):
        PR[s] = dot(lane(G, s), full(G), 0, 0).astype(BF)
    rend(7, srows(SR))
    pow_r = power(PR, SR, R, PR[...], 1)
    pr_home[z] = PR[z, :, mycols]
    prz = (lambda zz: PR.at[zz, :, mycols]), (lambda s: pr_home.at[s])
    zspread(8, *prz)
    iterate(pow_l, 0, IL)
    gmid(3, inter(DIR))
    gstart(4, inter(IL))
    iterate(pow_r, 1, IR)
    gstart(5, inter(IR))

    gend(3, inter(DIR))
    back = dot(full(DIR), R[q].reshape(2 * slab, 8 * slab), 1, 1).astype(BF)
    upd[z] = dot(rows(L), back, 1, 0).astype(BF).reshape(4, slab, width)

    def ucopy(t, h, right):
        zn = jnp.clip(z + 1 if right else z - 1, 0, 3)
        part = upd.at[t, h]
        return remote(part, part, (up_r if right else up_l).at[t, h], up_recv.at[t, h], at(zn, x, y, c))

    def upd_on(t, h, right):
        @pl.when(z < 3 if right else z > 0)
        def _():
            ucopy(t, h, right).start()

    for h in range(4):
        upd_on(z, h, True)
        upd_on(z, h, False)
    gmid(4, inter(IL))

    def refine(it, kind, out_s, home, zk):
        gend(kind, inter(it))
        gram = dot(rows(it), full(it), 1, 1).astype(BF)
        mine = it[:, x, :, mycols].reshape(half, width).astype(F32)
        new = 1.5 * mine - 0.5 * dot(gram, colb(it), 1, 0)
        out_s[...] = new.astype(BF).reshape(4, slab, width)
        home[z] = out_s[z]
        mv = tile_in(out_s, lambda s: home.at[s])
        return mv

    def relay(j, h):
        @pl.when(z - j >= 0)
        def _():
            t = jnp.maximum(z - j, 0)
            ucopy(t, h, True).wait_recv()
            upd_on(t, h, True)

        @pl.when(z + j <= 3)
        def _():
            t = jnp.minimum(z + j, 3)
            ucopy(t, h, False).wait_recv()
            upd_on(t, h, False)

    gmid(5, inter(IR))
    for h in range(4):
        relay(1, h)
    nlz = refine(IL, 4, nl_s, nl_home, 9)
    edge = jnp.logical_or(z == 0, z == 3)
    inside = jnp.logical_not(edge)
    zspread_if(edge, 9, *nlz)
    for h in range(4):
        relay(2, h)
    nrz = refine(IR, 5, nr_s, nr_home, 10)
    zspread_if(edge, 10, *nrz)

    def pick(who, h):
        got = jnp.zeros((slab, width), BF)
        for t in range(4):
            got = jnp.where(own_ref[t] == who, upd[t, h], got)
        return got

    def ucross(h, to):
        return remote(
            upd_px.at[h], upd_out.at[h, to], ux_sem.at[h], ux_sem.at[4 + h], xdev
        )

    for h in range(4):
        relay(3, h)
        upd_px[h] = pick(z * 2 + 1 - x, h)
        start(ucross(h, x))
    zspread_if(inside, 9, *nlz)
    zspread_if(inside, 10, *nrz)
    for h in range(4):
        upd_out[h, x] = pick(dp, h)
    for j in range(1, 8):
        dd = lax.rem(dp + j, 8)
        remote(pack_ref, norm_all.at[dd], nm_send.at[j], nm_recv.at[dd], (dd, q)).wait_recv()
    for j in range(8):
        nscr[0, 2 * j : 2 * j + 2] = norm_all[j, 16:18]
        nscr[1, 2 * j : 2 * j + 2] = norm_all[j, 18:20]
    total = jnp.sum(norm_all[:, 0:16], axis=0)
    nm = 0.9 * nscr[0] + 0.1 * total
    nv = 0.95 * nscr[1] + 0.05 * total * total
    step = nm / FIX_ONE / (jnp.sqrt(nv / FIX_TWO) + 1e-08)
    ns_out[...] = jnp.where(own_ref[nt] == dp, step, jnp.zeros_like(step))
    nscr[0] = nm
    nscr[1] = nv
    nm_out[...] = nscr[0, pl.ds(2 * dp, 2)]
    nv_out[...] = nscr[1, pl.ds(2 * dp, 2)]
    zwait(6, *rotz)
    zwait(7, *plz)
    zwait(8, *prz)
    zwait(9, *nlz)
    zwait(10, *nrz)
    for h in range(4):
        ucross(h, 1 - x).wait_recv()

    @pl.when(z < 3)
    def _():
        for j in range(4):
            @pl.when(z - j >= 0)
            def _():
                for h in range(4):
                    ucopy(jnp.maximum(z - j, 0), h, True).wait_send()

    @pl.when(z > 0)
    def _():
        for j in range(4):
            @pl.when(z + j <= 3)
            def _():
                for h in range(4):
                    ucopy(jnp.minimum(z + j, 3), h, False).wait_send()

    zsent(9, *nlz)
    zsent(10, *nrz)
    for cp in pending:
        cp.wait_send()


def finish_kernel(
    m1, m2, sl, sr, rot, prod_l, prod_r, new_l, new_r, slot, nm, nv, ns,
    m1_out, m2_out, sl_out, sr_out, bl_out, br_out, slot_out, nm_out, nv_out, ns_out,
):
    turned = rot[...].astype(F32)
    m1_out[...] = 0.9 * m1[...] + 0.1 * turned
    m2_out[...] = 0.95 * m2[...] + 0.05 * turned * turned
    sl_out[...] = 0.95 * sl[...] + 0.05 * prod_l[...].astype(F32)
    sr_out[...] = 0.95 * sr[...] + 0.05 * prod_r[...].astype(F32)
    bl_out[...] = new_l[...].astype(F32)
    br_out[...] = new_r[...].astype(F32)
    slot_out[...] = slot[...]
    nm_out[...] = nm[...]
    nv_out[...] = nv[...]
    ns_out[...] = ns[...]


def fused_shards(
    features,
    out_grads,
    norm_grads,
    owners,
    moment1,
    moment2,
    left_stats,
    right_stats,
    left_basis,
    right_basis,
    norm_m,
    norm_v,
):
    nt, slab, width = moment1.shape
    full = 8 * slab
    flat = out_grads.reshape(out_grads.shape[0], nt * width)
    vm = pl.BlockSpec(memory_space=pltpu.VMEM)
    hbm = pl.BlockSpec(memory_space=pl.ANY)
    home = jax.ShapeDtypeStruct((nt, slab, width), BF)
    big = pltpu.VMEM((4, 2, slab, full), BF)
    blk = pltpu.VMEM((4, slab, width), BF)
    piece = (4 * slab, width)
    dma = pltpu.SemaphoreType.DMA
    rot, prod_l, prod_r, new_l, new_r, slot, nm, nv, ns = pl.pallas_call(
        fused_kernel,
        out_shape=[home] * 5
        + [
            jax.ShapeDtypeStruct((4, 2, slab, width), BF),
            jax.ShapeDtypeStruct((2, 128), F32),
            jax.ShapeDtypeStruct((2, 128), F32),
            jax.ShapeDtypeStruct((16, 128), F32),
        ],
        in_specs=[hbm] * 2 + [vm] * 3 + [pl.BlockSpec(memory_space=pltpu.SMEM)] + [hbm] * 6,
        out_specs=[vm] * 9,
        scratch_shapes=[
            pltpu.VMEM(features.shape, BF),
            pltpu.VMEM(flat.shape, BF),
        ]
        + [pltpu.VMEM((nt, slab, width), F32)] * 6
        + [pltpu.VMEM((24, 128), F32), dma((8,))]
        + [
            pltpu.VMEM((4 * slab, features.shape[0]), BF),
            pltpu.VMEM((4,) + piece, BF),
            pltpu.VMEM((4,) + piece, F32),
            pltpu.VMEM((4,) + piece, BF),
            pltpu.VMEM((2, 4) + piece, BF),
            pltpu.VMEM((4,) + piece, BF),
        ]
        + [blk] * 6
        + [big] * 6
        + [pltpu.VMEM((4, slab, full), BF)] * 4
        + [blk] * 5
        + [pltpu.VMEM((4, 4, slab, width), BF), blk, pltpu.VMEM((2, 2, 8, width), F32)]
        + [
            dma((11, 4)), dma((11, 4)), dma((4,)), dma((4,)), dma((4,)), dma((2, 4)),
            dma((8, 6)), dma((8, 6)), dma((8, 5)), dma((8, 5)),
        ]
        + [pltpu.VMEM((8, 24, 128), F32), pltpu.VMEM((2, 16, 128), F32)]
        + [dma((4, 4)), dma((4, 4)), dma((4, 4)), dma((8,)), dma((8,)), dma((8,)), dma((2,)), dma((2,))],
        compiler_params=pltpu.CompilerParams(
            collective_id=0, has_side_effects=True, vmem_limit_bytes=56 * 2**20
        ),
        cost_estimate=pl.CostEstimate(flops=10**10, bytes_accessed=2**24, transcendentals=0),
    )(
        features, flat, norm_grads.reshape(16, 128), norm_m.reshape(2, 128), norm_v.reshape(2, 128), owners,
        moment1, moment2, left_stats, right_stats, left_basis, right_basis,
    )
    tile = pl.BlockSpec((2, slab, width), lambda i: (i, 0, 0))
    slots = pl.BlockSpec((2, 2, slab, width), lambda i: (i, 0, 0, 0))
    once2 = pl.BlockSpec((2, 128), lambda i: (0, 0))
    once16 = pl.BlockSpec((16, 128), lambda i: (0, 0))
    state = jax.ShapeDtypeStruct((nt, slab, width), F32)
    outs = pl.pallas_call(
        finish_kernel,
        grid=(nt // 2,),
        out_shape=[state] * 6
        + [
            jax.ShapeDtypeStruct((4, 2, slab, width), BF),
            jax.ShapeDtypeStruct((2, 128), F32),
            jax.ShapeDtypeStruct((2, 128), F32),
            jax.ShapeDtypeStruct((16, 128), F32),
        ],
        in_specs=[tile] * 9 + [slots, once2, once2, once16],
        out_specs=[tile] * 6 + [slots, once2, once2, once16],
        cost_estimate=pl.CostEstimate(flops=2**20, bytes_accessed=2**23, transcendentals=0),
    )(moment1, moment2, left_stats, right_stats, rot, prod_l, prod_r, new_l, new_r, slot, nm, nv, ns)
    slot, nm, nv, ns = outs[6:]
    return (
        *outs[:6],
        slot.reshape(1, full, width),
        nm.reshape(norm_m.shape),
        nv.reshape(norm_v.shape),
        ns.reshape(1, -1),
    )


def solution(mesh):
    in_specs = (
        P("dp", None),
        P("dp", None, "mp"),
        P("dp", None),
        P(),
        P(None, "dp", "mp"),
        P(None, "dp", "mp"),
        P(None, "dp", "mp"),
        P(None, "dp", "mp"),
        P(None, "dp", "mp"),
        P(None, "dp", "mp"),
        P("dp"),
        P("dp"),
    )
    out_specs = (
        P(None, "dp", "mp"),
        P(None, "dp", "mp"),
        P(None, "dp", "mp"),
        P(None, "dp", "mp"),
        P(None, "dp", "mp"),
        P(None, "dp", "mp"),
        P("dp", None, "mp"),
        P("dp"),
        P("dp"),
        P("dp", None),
    )
    fused = mesh.shape["dp"] == 8 and mesh.shape["mp"] == 4
    body = fused_shards if fused else shards
    return jax.shard_map(body, mesh=mesh, in_specs=in_specs, out_specs=out_specs, check_vma=False)
```
